128 devices in a mesh: dev: 128 (over y, z, x, core).
Axes of the slice: x: 4, y: 4, z: 4, core: 2. Of those that a mesh axis runs over, the one named last changes fastest.
Arguments:
- micrographs: bfloat16 [512, 1024, 1024], P('dev'), may hold values from -32 to 32
- positions: int32 [2, 512, 64], P(None, 'dev'), may hold values from 0 to 960
- counts: int32 [512], P('dev'), may hold values from 0 to 64, as said below
- dest_rows: int32 [512, 64], P('dev'), may hold values from -1 to 16383, as said below
- templates: bfloat16 [100, 32, 128], replicated, may hold values from -1 to 1
Outputs:
- class_means: float32 [100, 32, 128], replicated
- loglik: float32 [16384], P('dev')
The draws below stay inside these ranges and needn't reach their ends.
Inputs may be any that keep to these rules, and one draw needn't show every extreme that they name: All counts sum to 16384; the counts of one device sum to at most 256, and some device's counts reach it. `dest_rows`: slot j of micrograph i holds -1 when j >= counts[i], else a row; every row of 0 to 16383 occurs once over all devices. The rows held by one device fall at most 2 times into the rows d * 128 to (d + 1) * 128 - 1 of any one device d, and some device reaches 2 with every device.
All inputs are finite; a program needn't handle non-finite values.
Results may differ from the reference program's by a relative error of at most 0.0055.
The reference program's roundings to bfloat16 on the way count: a program that leaves them out, or rounds other values in their place, can miss the bound.
Values may be sent and summed in bfloat16 or wider, within the bound.
A program may use at most 192 MiB of HBM per device.

```python
import jax
import jax.numpy as jnp
from jax import lax

BOX = 64
RAD = 32
ANG = 128
CLASSES = 100
ROTS = 36
MIC_DEV = 4
MAXP = 64
MIC_PIX = 1024
PART_DEV = 128
MICS = 512
PARTICLES = 16384
N_DEV = 128


def routing_plan(key):
    source_slots = MIC_DEV * MAXP
    first_key, second_key, third_key = jax.random.split(jax.random.fold_in(key, 7), 3)
    busiest = jax.random.randint(first_key, (), 0, N_DEV)
    shuffled = jax.random.permutation(second_key, (N_DEV - 1) * source_slots)
    slot_ids = jnp.arange(N_DEV * source_slots, dtype=jnp.int32)
    owner = slot_ids // source_slots
    others = slot_ids - source_slots * (owner > busiest).astype(jnp.int32)
    others = jnp.where(owner == busiest, 0, others)
    chosen = (owner == busiest) | (shuffled[others] < N_DEV * PART_DEV - source_slots)
    counts = jnp.sum(chosen.reshape(MICS, MAXP).astype(jnp.int32), axis=1)
    present = (jnp.arange(MAXP, dtype=jnp.int32)[None, :] < counts[:, None]).reshape(N_DEV, source_slots)
    keyed = jax.random.randint(third_key, (N_DEV, source_slots), 0, 2 ** 20) * source_slots
    keyed = keyed + jnp.arange(source_slots, dtype=jnp.int32)[None, :]
    keyed = jnp.where(present, keyed, keyed + 2 ** 30)
    ranking = jnp.argsort(jnp.argsort(keyed, axis=1), axis=1).astype(jnp.int32)
    per_device = jnp.sum(present.astype(jnp.int32), axis=1)
    starts = jnp.cumsum(per_device) - per_device
    ranks = starts[:, None] + ranking
    rows = ranks % N_DEV * PART_DEV + ranks // N_DEV
    rows = jnp.where(present, rows, -1).reshape(MICS, MAXP).astype(jnp.int32)
    return (counts.astype(jnp.int32), rows)


def draw_counts(key, part):
    return routing_plan(key)[0]


def draw_dest_rows(key, part):
    return routing_plan(key)[1]


def draw_micrographs(key, part):
    scale_key, noise_key = jax.random.split(key)
    scales = jnp.exp(jax.random.uniform(scale_key, (MICS, 1, 1), minval=jnp.log(0.5), maxval=jnp.log(2.0)))
    noise = jnp.clip(jax.random.normal(noise_key, (MICS, MIC_PIX, MIC_PIX)), -4.0, 4.0)
    return (scales * noise).astype(jnp.bfloat16)


def draw_templates(key, part):
    scale_key, noise_key = jax.random.split(jax.random.fold_in(key, 3))
    scales = jnp.exp(jax.random.uniform(scale_key, (CLASSES, 1, 1), minval=jnp.log(0.05), maxval=jnp.log(0.2)))
    noise = jnp.clip(jax.random.normal(noise_key, (CLASSES, RAD, ANG)), -4.0, 4.0)
    return (scales * noise).astype(jnp.bfloat16)


def place_ends(drawn, stream_key, low, high):
    longest = drawn.shape.index(max(drawn.shape))
    spots = []
    for shift in (0, 1):
        where = [jax.random.randint(jax.random.fold_in(stream_key, axis), (), 0, length) for axis, length in enumerate(drawn.shape)]
        where[longest] = (where[longest] + shift) % drawn.shape[longest]
        spots.append(tuple(where))
    return drawn.at[spots[0]].set(low).at[spots[1]].set(high)


def setup_inputs(seed: int = 0) -> dict:
    key_list = jax.random.split(jax.random.key(seed), 6)
    micrographs = draw_micrographs(jax.random.fold_in(key_list[5], 71), 0)
    positions = place_ends(jax.random.randint(key_list[1], (2, MICS, MAXP), 0, MIC_PIX - BOX + 1), jax.random.fold_in(key_list[1], 1), 0, MIC_PIX - BOX).astype(jnp.int32)
    counts = draw_counts(jax.random.fold_in(key_list[5], 71), 0)
    dest_rows = draw_dest_rows(jax.random.fold_in(key_list[5], 71), 0)
    templates = draw_templates(jax.random.fold_in(key_list[5], 71), 0)
    return dict(micrographs=micrographs, positions=positions, counts=counts, dest_rows=dest_rows, templates=templates)


def polar_table():
    center = (BOX - 1) / 2.0
    radius = (jnp.arange(RAD, dtype=jnp.float32) + 0.5) * (BOX / 2.0 - 1.0) / RAD
    theta = 2.0 * jnp.pi * jnp.arange(ANG, dtype=jnp.float32) / ANG
    row_pos = (center + radius[:, None] * jnp.sin(theta)[None, :]).reshape(-1)
    col_pos = (center + radius[:, None] * jnp.cos(theta)[None, :]).reshape(-1)
    pixels = jnp.arange(BOX, dtype=jnp.float32)
    row_weight = jnp.maximum(0.0, 1.0 - jnp.abs(pixels[:, None] - row_pos[None, :]))
    col_weight = jnp.maximum(0.0, 1.0 - jnp.abs(pixels[:, None] - col_pos[None, :]))
    table = row_weight[:, None, :] * col_weight[None, :, :]
    return table.reshape(BOX * BOX, RAD * ANG).astype(jnp.bfloat16)


def rotation_table():
    angles = jnp.arange(ANG, dtype=jnp.float32)
    shifts = jnp.arange(ROTS, dtype=jnp.float32) * ANG / ROTS
    offset = angles[None, :, None] - angles[None, None, :] - shifts[:, None, None]
    offset = offset - ANG * jnp.floor(offset / ANG + 0.5)
    return jnp.maximum(0.0, 1.0 - jnp.abs(offset)).astype(jnp.bfloat16)


def cut_box(pictures, which, row_start, col_start):
    return lax.dynamic_slice(pictures, (which, row_start, col_start), (1, BOX, BOX))[0]


def reference(micrographs, positions, counts, dest_rows, templates):
    mic_index = jnp.repeat(jnp.arange(MICS, dtype=jnp.int32), MAXP)
    boxes = jax.vmap(cut_box, in_axes=(None, 0, 0, 0))(
        micrographs, mic_index, positions[0].reshape(-1).astype(jnp.int32), positions[1].reshape(-1).astype(jnp.int32))
    boxes = boxes.reshape(MICS * MAXP, BOX * BOX)
    present = (jnp.arange(MAXP, dtype=jnp.int32)[None, :] < counts[:, None]).reshape(-1)
    targets = dest_rows.reshape(-1)
    landing = jnp.where(present & (targets >= 0), targets, PARTICLES).astype(jnp.int32)
    balanced = jnp.zeros((PARTICLES, BOX * BOX), boxes.dtype).at[landing].set(boxes, mode="drop")
    table = polar_table()
    polar = jnp.dot(balanced.astype(jnp.float32), table.astype(jnp.float32),
                    preferred_element_type=jnp.float32).astype(jnp.bfloat16)
    rotations = rotation_table().astype(jnp.float32)
    rotated = jnp.einsum("kab,crb->ckra", rotations, templates.astype(jnp.float32)).astype(jnp.bfloat16)
    rotated_flat = rotated.reshape(CLASSES * ROTS, RAD * ANG).astype(jnp.float32)
    energy = 0.5 * jnp.sum(rotated_flat * rotated_flat, axis=1)
    polar_wide = polar.astype(jnp.float32)
    scores = jnp.dot(polar_wide, rotated_flat.T, preferred_element_type=jnp.float32) - energy[None, :]
    peak_score = jnp.max(scores, axis=1, keepdims=True)
    loglik = peak_score[:, 0] + jnp.log(jnp.sum(jnp.exp(scores - peak_score), axis=1))
    weights = jnp.exp(scores - loglik[:, None]).astype(jnp.bfloat16).astype(jnp.float32)
    totals = jnp.sum(weights, axis=0).reshape(CLASSES, ROTS).sum(axis=1)
    gathered = jnp.dot(weights.T, polar_wide, preferred_element_type=jnp.float32)
    class_sums = jnp.einsum("ckra,kab->crb", gathered.reshape(CLASSES, ROTS, RAD, ANG), rotations,
                            precision=lax.Precision.HIGHEST)
    class_means = class_sums / jnp.maximum(totals, 1.0)[:, None, None]
    return (class_means, loglik)
```

```python
import functools
import numpy as np
import jax
import jax.numpy as jnp
from jax import lax
from jax.experimental import pallas as pl
from jax.experimental.pallas import tpu as pltpu

BOX = 64
RAD = 32
ANG = 128
CLASSES = 100
ROTS = 36
CPAD = 104
QROT = 4
BASE = 9
NROWS = 4 * 2 * CPAD + 112
F32 = jnp.float32
BF16 = jnp.bfloat16


def sample_points():
    center = np.float32((BOX - 1) / 2.0)
    radius = (np.arange(RAD, dtype=np.float32) + np.float32(0.5)) * np.float32(BOX / 2.0 - 1.0) / np.float32(RAD)
    theta = np.float32(2.0 * np.pi) * np.arange(ANG, dtype=np.float32) / np.float32(ANG)
    ys = (center + radius[:, None] * np.sin(theta)[None, :]).reshape(1, -1)
    xs = (center + radius[:, None] * np.cos(theta)[None, :]).reshape(1, -1)
    return ys.astype(np.float32), xs.astype(np.float32)


def rotation_taps():
    a = np.arange(ANG, dtype=np.float32)
    taps = []
    for k in range(BASE):
        shift = np.float32(k) * np.float32(ANG) / np.float32(ROTS)
        d = a - np.float32(0) - shift
        d = d - ANG * np.floor(d / np.float32(ANG) + np.float32(0.5))
        w = np.maximum(np.float32(0), np.float32(1) - np.abs(d)).astype(jnp.bfloat16).astype(np.float32)
        first = int(32 * k // 9)
        taps.append((first, float(w[first]), float(w[(first + 1) % ANG]) if k else 0.0))
    return taps


TAPS = rotation_taps()


def local_kernel(pos, counts, mic, dest, ys, xs, tmpl, g_out, tot_out, ll_out,
                 raw, planes, flat, boxes, wtile, tflat, rot, esum, shifted, scores, weights, tsum, sems):
    mics = mic.shape[0]
    slots = pos.shape[2]
    parts = mics * slots

    def fetch(i):
        return pltpu.make_async_copy(mic.at[i], raw.at[i % 2], sems.at[i % 2])

    fetch(0).start()
    fetch(1).start()

    lane1 = lax.broadcasted_iota(jnp.int32, (1, ANG), 1)

    tflat[pl.ds(CLASSES * RAD, (CPAD - CLASSES) * RAD), :] = jnp.zeros(((CPAD - CLASSES) * RAD, ANG), F32)
    tflat[pl.ds(0, CLASSES * RAD), :] = tmpl[...].reshape(CLASSES * RAD, ANG).astype(F32)
    esum[...] = jnp.zeros_like(esum)
    rot[pl.ds(8 * CPAD, 112), :] = jnp.zeros((112, RAD * ANG), BF16)

    def rotate_radius(r, _):
        x = tflat[pl.ds(r, CPAD, stride=RAD), :]
        x1 = pltpu.roll(x, 1, 1)
        col = pl.ds(pl.multiple_of(r * ANG, ANG), ANG)
        turned = []
        for first, w0, w1 in TAPS:
            y = x if w1 == 0.0 else w0 * x + w1 * x1
            turned.append(pltpu.roll(y, first, 1) if first else y)
        turned.append(jnp.zeros((8, ANG), F32))
        for i in range(0, BASE, 2):
            pair = jnp.concatenate(turned[i : i + 2], axis=0).astype(BF16)
            rot[pl.ds(i * CPAD, pair.shape[0]), col] = pair
            wide = pair.astype(F32)
            esum[pl.ds(i * CPAD, pair.shape[0]), :] += wide * wide
        return 0

    lax.fori_loop(0, RAD, rotate_radius, 0)

    lanes = lax.broadcasted_iota(jnp.int32, (BOX // 2, ANG), 1)
    for i in range(mics):
        fetch(i).wait()
        for t in range(8):
            planes[t, :, :] = raw[i % 2, :, t * ANG : (t + 1) * ANG].astype(F32)
        if i + 2 < mics:
            fetch(i + 2).start()

        def cut(j, _, i=i):
            y = pos[0, i, j]
            x = pos[1, i, j]
            t = x // ANG
            s = x - t * ANG
            t1 = jnp.minimum(t + 1, 7)
            even = pl.ds(y, BOX // 2, stride=2)
            odd = pl.ds(y + 1, BOX // 2, stride=2)
            keep = lanes >= s
            e = jnp.where(keep, planes[t, even, :], planes[t1, even, :])
            o = jnp.where(keep, planes[t, odd, :], planes[t1, odd, :])
            e = pltpu.roll(e, lax.rem(ANG - s, ANG), 1)
            o = pltpu.roll(o, lax.rem(ANG + BOX - s, ANG), 1)
            flat[pl.ds(i * slots + j, BOX // 2, stride=parts), :] = jnp.where(lanes < BOX, e, o)
            return 0

        lax.fori_loop(0, slots, cut, 0, unroll=4)

    for s in range(BOX // 2):
        boxes[:, s * ANG : (s + 1) * ANG] = flat[pl.ds(s * parts, parts), :].astype(BF16)

    pix = lax.broadcasted_iota(jnp.int32, (BOX, 2 * ANG), 0).astype(F32)
    for g in range(RAD // 2):
        radius = (2 * g + 1.5) * (BOX / 2.0 - 1.0) / RAD
        low = int(np.floor(31.5 - radius)) - 1
        low = max(0, low // 4 * 4)
        high = BOX - low
        cols = slice(g * 2 * ANG, (g + 1) * 2 * ANG)
        rw = jnp.maximum(0.0, 1.0 - jnp.abs(pix - ys[:, cols]))
        cw = jnp.maximum(0.0, 1.0 - jnp.abs(pix - xs[:, cols]))
        w = wtile.at[g % 2]
        for u in range(low, high):
            w[u * BOX : (u + 1) * BOX, :] = (rw[u : u + 1, :] * cw).astype(BF16)
        p = jnp.dot(boxes[:, low * BOX : high * BOX], w[low * BOX : high * BOX, :], preferred_element_type=F32)
        for h in range(2):
            half = p[:, h * ANG : (h + 1) * ANG]
            c0 = (2 * g + h) * ANG
            for j in range(QROT):
                part = half if j == 0 else pltpu.roll(half, ANG - 32 * j, 1)
                shifted[j * parts : (j + 1) * parts, c0 : c0 + ANG] = part.astype(BF16)

    rows = lax.broadcasted_iota(jnp.int32, (NROWS, 1), 0)
    energy = 0.5 * jnp.sum(esum[...], axis=1, keepdims=True)
    pad = (lax.rem(rows, CPAD) >= CLASSES) | (rows >= BASE * CPAD)
    energy = jnp.where(pad, 1e30, energy)

    def score(j, peak):
        rows_j = pl.ds(pl.multiple_of(j * parts, parts), parts)
        prod = lax.dot_general(rot[...], shifted[rows_j, :], (((1,), (1,)), ((), ())), preferred_element_type=F32)
        prod = prod - energy
        scores[:, rows_j] = prod
        return jnp.maximum(peak, jnp.max(prod, axis=0, keepdims=True))

    peak = lax.fori_loop(0, QROT, score, jnp.full((1, parts), -3e38, F32))
    peak4 = jnp.concatenate([peak] * QROT, axis=1)

    def expo(n, acc):
        rr = pl.ds(pl.multiple_of(n * 16, 16), 16)
        e = jnp.exp(scores[rr, :] - peak4)
        scores[rr, :] = e
        return acc + e[:8] + e[8:]

    acc = lax.fori_loop(0, NROWS // 16, expo, jnp.zeros((8, QROT * parts), F32))
    norm = jnp.sum(acc, axis=0, keepdims=True)
    norm = sum(norm[:, j * parts : (j + 1) * parts] for j in range(QROT))
    loglik = peak + jnp.log(norm)

    lane = lax.broadcasted_iota(jnp.int32, (1, parts), 1)
    target = dest[...]
    live = target >= 0
    for i in range(mics):
        live = live & ((lane < i * slots + counts[i]) | (lane >= (i + 1) * slots))
    inv = jnp.where(live, 1.0 / norm, 0.0)
    inv4 = jnp.concatenate([inv] * QROT, axis=1)

    def weigh(n, _):
        rr = pl.ds(pl.multiple_of(n * 16, 16), 16)
        w = (scores[rr, :] * inv4).astype(BF16)
        weights[rr, :] = w
        wide = w.astype(F32)
        tsum[rr, :] = sum(wide[:, k * ANG : (k + 1) * ANG] for k in range(QROT * parts // ANG))
        return 0

    lax.fori_loop(0, NROWS // 16, weigh, 0)
    tot = jnp.sum(tsum[...], axis=1, keepdims=True)
    tot = sum(tot[i * CPAD : (i + 1) * CPAD] for i in range(BASE))
    spot = lax.broadcasted_iota(jnp.int32, (CPAD, ANG), 0) == lax.broadcasted_iota(jnp.int32, (CPAD, ANG), 1)
    tot_out[...] = jnp.sum(jnp.where(spot, tot, 0.0), axis=0, keepdims=True)

    which = lax.broadcasted_iota(jnp.int32, (ANG, parts), 0)
    owner = jnp.where((which == (target >> 7)) & live, 1.0, 0.0)
    row = jnp.where(which == (target & 127), 1.0, 0.0).astype(BF16)
    rest = loglik
    table = jnp.zeros((ANG, ANG), F32)
    for _ in range(3):
        piece = rest.astype(BF16).astype(F32)
        table += lax.dot_general((owner * piece).astype(BF16), row, (((1,), (1,)), ((), ())), preferred_element_type=F32)
        rest = rest - piece
    ll_out[...] = table

    def collect(g, _):
        cols = pl.ds(pl.multiple_of(g * 2 * ANG, 2 * ANG), 2 * ANG)
        h = jnp.dot(weights[...], shifted[:, cols], preferred_element_type=F32)
        for k in range(2):
            sum0 = jnp.zeros((CPAD, ANG), F32)
            sum1 = jnp.zeros((CPAD, ANG), F32)
            for i, (first, w0, w1) in enumerate(TAPS):
                q = h[i * CPAD : (i + 1) * CPAD, k * ANG : (k + 1) * ANG]
                if first:
                    q = pltpu.roll(q, ANG - first, 1)
                sum0 += w0 * q
                if w1:
                    sum1 += w1 * q
            g_out[2 * g + k, :, :] = sum0 + pltpu.roll(sum1, ANG - 1, 1)
        return 0

    lax.fori_loop(0, RAD // 2, collect, 0)


def local_terms(micrographs, positions, counts, dest_rows, templates):
    mics, slots = dest_rows.shape
    parts = mics * slots
    cells = RAD * ANG
    ys, xs = sample_points()
    vmem = pl.BlockSpec(memory_space=pltpu.VMEM)
    smem = pl.BlockSpec(memory_space=pltpu.SMEM)
    return pl.pallas_call(
        local_kernel,
        out_shape=(
            jax.ShapeDtypeStruct((RAD, CPAD, ANG), F32),
            jax.ShapeDtypeStruct((1, ANG), F32),
            jax.ShapeDtypeStruct((ANG, ANG), F32),
        ),
        in_specs=[smem, smem, pl.BlockSpec(memory_space=pl.ANY), vmem, vmem, vmem, vmem],
        out_specs=(vmem, vmem, vmem),
        scratch_shapes=[
            pltpu.VMEM((2, 1024, 1024), BF16),
            pltpu.VMEM((8, 1024, ANG), F32),
            pltpu.VMEM((BOX // 2 * parts, ANG), F32),
            pltpu.VMEM((parts, BOX * BOX), BF16),
            pltpu.VMEM((2, BOX * BOX, 2 * ANG), BF16),
            pltpu.VMEM((CPAD * RAD, ANG), F32),
            pltpu.VMEM((NROWS, cells), BF16),
            pltpu.VMEM((NROWS, ANG), F32),
            pltpu.VMEM((QROT * parts, cells), BF16),
            pltpu.VMEM((NROWS, QROT * parts), F32),
            pltpu.VMEM((NROWS, QROT * parts), BF16),
            pltpu.VMEM((NROWS, ANG), F32),
            pltpu.SemaphoreType.DMA((2,)),
        ],
        compiler_params=pltpu.CompilerParams(vmem_limit_bytes=60 * 1024 * 1024),
        name="local_terms",
    )(positions, counts, micrographs, dest_rows.reshape(1, parts), jnp.asarray(ys), jnp.asarray(xs), templates)


DEVICES = 128


def on_device(micrographs, positions, counts, dest_rows, templates):
    sums, tot, table = local_terms(micrographs, positions, counts, dest_rows, templates)
    packed = jnp.concatenate([sums.reshape(-1, ANG), tot, table], axis=0)
    packed = lax.psum(packed, "dev")
    sums = packed[: RAD * CPAD].reshape(RAD, CPAD, ANG)[:, :CLASSES]
    tot = packed[RAD * CPAD, :CLASSES]
    means = sums.transpose(1, 0, 2) / jnp.maximum(tot, 1.0)[:, None, None]
    table = packed[RAD * CPAD + 1 :]
    mine = lax.dynamic_slice(table, (lax.axis_index("dev"), 0), (1, ANG))[0]
    return means, mine


def solution(mesh):
    P = jax.sharding.PartitionSpec
    return jax.shard_map(
        on_device,
        mesh=mesh,
        in_specs=(P("dev", None, None), P(None, "dev", None), P("dev"), P("dev", None), P()),
        out_specs=(P(), P("dev")),
        check_vma=False,
    )
```

```python
import functools
import numpy as np
import jax
import jax.numpy as jnp
from jax import lax
from jax.experimental import pallas as pl
from jax.experimental.pallas import tpu as pltpu

BOX = 64
RAD = 32
ANG = 128
CLASSES = 100
ROTS = 36
CPAD = 104
QROT = 4
BASE = 9
NROWS = 4 * 2 * CPAD + 112
DEVICES = 128
CHIPS = DEVICES // 2
PIECE = 32
F32 = jnp.float32
BF16 = jnp.bfloat16


def sample_points():
    center = np.float32((BOX - 1) / 2.0)
    radius = (np.arange(RAD, dtype=np.float32) + np.float32(0.5)) * np.float32(BOX / 2.0 - 1.0) / np.float32(RAD)
    theta = np.float32(2.0 * np.pi) * np.arange(ANG, dtype=np.float32) / np.float32(ANG)
    ys = (center + radius[:, None] * np.sin(theta)[None, :]).reshape(1, -1)
    xs = (center + radius[:, None] * np.cos(theta)[None, :]).reshape(1, -1)
    return ys.astype(np.float32), xs.astype(np.float32)


def rotation_taps():
    a = np.arange(ANG, dtype=np.float32)
    taps = []
    for k in range(BASE):
        shift = np.float32(k) * np.float32(ANG) / np.float32(ROTS)
        d = a - np.float32(0) - shift
        d = d - ANG * np.floor(d / np.float32(ANG) + np.float32(0.5))
        w = np.maximum(np.float32(0), np.float32(1) - np.abs(d)).astype(jnp.bfloat16).astype(np.float32)
        first = int(32 * k // 9)
        taps.append((first, float(w[first]), float(w[(first + 1) % ANG]) if k else 0.0))
    return taps


TAPS = rotation_taps()


def local_kernel(pos, counts, mic, dest, ys, xs, tmpl, out, extra, raw, planes, flat, boxes, wtile, tflat, rot, esum, shifted, scores, weights, tsum, sems):
    mics = mic.shape[0]
    slots = pos.shape[2]
    parts = mics * slots

    def fetch(i):
        return pltpu.make_async_copy(mic.at[i], raw.at[i % 2], sems.at[i % 2])

    fetch(0).start()
    fetch(1).start()

    lane1 = lax.broadcasted_iota(jnp.int32, (1, ANG), 1)

    tflat[pl.ds(CLASSES * RAD, (CPAD - CLASSES) * RAD), :] = jnp.zeros(((CPAD - CLASSES) * RAD, ANG), F32)
    tflat[pl.ds(0, CLASSES * RAD), :] = tmpl[...].reshape(CLASSES * RAD, ANG).astype(F32)
    esum[...] = jnp.zeros_like(esum)
    rot[pl.ds(8 * CPAD, 112), :] = jnp.zeros((112, RAD * ANG), BF16)

    def rotate_radius(r, _):
        x = tflat[pl.ds(r, CPAD, stride=RAD), :]
        x1 = pltpu.roll(x, 1, 1)
        col = pl.ds(pl.multiple_of(r * ANG, ANG), ANG)
        turned = []
        for first, w0, w1 in TAPS:
            y = x if w1 == 0.0 else w0 * x + w1 * x1
            turned.append(pltpu.roll(y, first, 1) if first else y)
        turned.append(jnp.zeros((8, ANG), F32))
        for i in range(0, BASE, 2):
            pair = jnp.concatenate(turned[i : i + 2], axis=0).astype(BF16)
            rot[pl.ds(i * CPAD, pair.shape[0]), col] = pair
            wide = pair.astype(F32)
            esum[pl.ds(i * CPAD, pair.shape[0]), :] += wide * wide
        return 0

    lax.fori_loop(0, RAD, rotate_radius, 0)

    lanes = lax.broadcasted_iota(jnp.int32, (BOX // 2, ANG), 1)
    for i in range(mics):
        fetch(i).wait()
        for t in range(8):
            planes[t, :, :] = raw[i % 2, :, t * ANG : (t + 1) * ANG].astype(F32)
        if i + 2 < mics:
            fetch(i + 2).start()

        def cut(j, _, i=i):
            y = pos[0, i, j]
            x = pos[1, i, j]
            t = x // ANG
            s = x - t * ANG
            t1 = jnp.minimum(t + 1, 7)
            even = pl.ds(y, BOX // 2, stride=2)
            odd = pl.ds(y + 1, BOX // 2, stride=2)
            keep = lanes >= s
            e = jnp.where(keep, planes[t, even, :], planes[t1, even, :])
            o = jnp.where(keep, planes[t, odd, :], planes[t1, odd, :])
            e = pltpu.roll(e, lax.rem(ANG - s, ANG), 1)
            o = pltpu.roll(o, lax.rem(ANG + BOX - s, ANG), 1)
            flat[pl.ds(i * slots + j, BOX // 2, stride=parts), :] = jnp.where(lanes < BOX, e, o)
            return 0

        lax.fori_loop(0, slots, cut, 0, unroll=4)

    for s in range(BOX // 2):
        boxes[:, s * ANG : (s + 1) * ANG] = flat[pl.ds(s * parts, parts), :].astype(BF16)

    pix = lax.broadcasted_iota(jnp.int32, (BOX, 2 * ANG), 0).astype(F32)
    for g in range(RAD // 2):
        radius = (2 * g + 1.5) * (BOX / 2.0 - 1.0) / RAD
        low = int(np.floor(31.5 - radius)) - 1
        low = max(0, low // 4 * 4)
        high = BOX - low
        cols = slice(g * 2 * ANG, (g + 1) * 2 * ANG)
        rw = jnp.maximum(0.0, 1.0 - jnp.abs(pix - ys[:, cols]))
        cw = jnp.maximum(0.0, 1.0 - jnp.abs(pix - xs[:, cols]))
        w = wtile.at[g % 2]
        for u in range(low, high):
            w[u * BOX : (u + 1) * BOX, :] = (rw[u : u + 1, :] * cw).astype(BF16)
        p = jnp.dot(boxes[:, low * BOX : high * BOX], w[low * BOX : high * BOX, :], preferred_element_type=F32)
        for h in range(2):
            half = p[:, h * ANG : (h + 1) * ANG]
            c0 = (2 * g + h) * ANG
            for j in range(QROT):
                part = half if j == 0 else pltpu.roll(half, ANG - 32 * j, 1)
                shifted[j * parts : (j + 1) * parts, c0 : c0 + ANG] = part.astype(BF16)

    rows = lax.broadcasted_iota(jnp.int32, (NROWS, 1), 0)
    energy = 0.5 * jnp.sum(esum[...], axis=1, keepdims=True)
    pad = (lax.rem(rows, CPAD) >= CLASSES) | (rows >= BASE * CPAD)
    energy = jnp.where(pad, 1e30, energy)

    def score(j, peak):
        rows_j = pl.ds(pl.multiple_of(j * parts, parts), parts)
        prod = lax.dot_general(rot[...], shifted[rows_j, :], (((1,), (1,)), ((), ())), preferred_element_type=F32)
        prod = prod - energy
        scores[:, rows_j] = prod
        return jnp.maximum(peak, jnp.max(prod, axis=0, keepdims=True))

    peak = lax.fori_loop(0, QROT, score, jnp.full((1, parts), -3e38, F32))
    peak4 = jnp.concatenate([peak] * QROT, axis=1)

    def expo(n, acc):
        rr = pl.ds(pl.multiple_of(n * 16, 16), 16)
        e = jnp.exp(scores[rr, :] - peak4)
        scores[rr, :] = e
        return acc + e[:8] + e[8:]

    acc = lax.fori_loop(0, NROWS // 16, expo, jnp.zeros((8, QROT * parts), F32))
    norm = jnp.sum(acc, axis=0, keepdims=True)
    norm = sum(norm[:, j * parts : (j + 1) * parts] for j in range(QROT))
    loglik = peak + jnp.log(norm)

    lane = lax.broadcasted_iota(jnp.int32, (1, parts), 1)
    target = dest[...]
    live = target >= 0
    for i in range(mics):
        live = live & ((lane < i * slots + counts[i]) | (lane >= (i + 1) * slots))
    inv = jnp.where(live, 1.0 / norm, 0.0)
    inv4 = jnp.concatenate([inv] * QROT, axis=1)

    def weigh(n, _):
        rr = pl.ds(pl.multiple_of(n * 16, 16), 16)
        w = (scores[rr, :] * inv4).astype(BF16)
        weights[rr, :] = w
        wide = w.astype(F32)
        tsum[rr, :] = sum(wide[:, k * ANG : (k + 1) * ANG] for k in range(QROT * parts // ANG))
        return 0

    lax.fori_loop(0, NROWS // 16, weigh, 0)
    tot = jnp.sum(tsum[...], axis=1, keepdims=True)
    tot = sum(tot[i * CPAD : (i + 1) * CPAD] for i in range(BASE))
    spot = lax.broadcasted_iota(jnp.int32, (CPAD, ANG), 0) == lax.broadcasted_iota(jnp.int32, (CPAD, ANG), 1)
    tot = jnp.sum(jnp.where(spot, tot, 0.0), axis=0, keepdims=True)
    high = tot.astype(BF16).astype(F32)
    first = lax.rem(lax.axis_index("dev"), 2) == 0
    extra[...] = jnp.zeros_like(extra)
    for value, here, there in ((high, 1, 6), (tot - high, 2, 7)):
        value = jnp.broadcast_to(value, (DEVICES, ANG))
        extra[pl.ds(here, DEVICES, stride=8), :] = jnp.where(first, value, 0.0)
        extra[pl.ds(there, DEVICES, stride=8), :] = jnp.where(first, 0.0, value)

    which = lax.broadcasted_iota(jnp.int32, (ANG, parts), 0)
    owner = jnp.where((which == (target >> 7)) & live, 1.0, 0.0)
    row = jnp.where(which == (target & 127), 1.0, 0.0).astype(BF16)
    rest = loglik
    for k in range(3):
        piece = rest.astype(BF16).astype(F32)
        table = lax.dot_general((owner * piece).astype(BF16), row, (((1,), (1,)), ((), ())), preferred_element_type=F32)
        extra[pl.ds(3 + k, DEVICES, stride=8), :] = table
        rest = rest - piece

    top = lax.broadcasted_iota(jnp.int32, (8, ANG), 0)

    def collect(g, _):
        cols = pl.ds(pl.multiple_of(g * 2 * ANG, 2 * ANG), 2 * ANG)
        h = jnp.dot(weights[...], shifted[:, cols], preferred_element_type=F32)
        for k in range(2):
            sum0 = jnp.zeros((CPAD, ANG), F32)
            sum1 = jnp.zeros((CPAD, ANG), F32)
            for i, (first, w0, w1) in enumerate(TAPS):
                q = h[i * CPAD : (i + 1) * CPAD, k * ANG : (k + 1) * ANG]
                if first:
                    q = pltpu.roll(q, ANG - first, 1)
                sum0 += w0 * q
                if w1:
                    sum1 += w1 * q
            total = sum0 + pltpu.roll(sum1, ANG - 1, 1)
            r = 2 * g + k
            for q in range(4):
                tail = total[96:] if q == 0 else pltpu.roll(total[96:], 8 - q, 0)
                spare = extra[pl.ds(pl.multiple_of((4 * r + q) * 8, 8), 8), :]
                tail = jnp.where(top == 0, tail, spare)
                piece = jnp.concatenate([total[24 * q : 24 * q + 24], tail], axis=0)
                out[q % 2, 2 * r + q // 2, :, :] = piece.astype(BF16)
        return 0

    lax.fori_loop(0, RAD // 2, collect, 0)


def local_terms(micrographs, positions, counts, dest_rows, templates):
    mics, slots = dest_rows.shape
    parts = mics * slots
    cells = RAD * ANG
    ys, xs = sample_points()
    vmem = pl.BlockSpec(memory_space=pltpu.VMEM)
    smem = pl.BlockSpec(memory_space=pltpu.SMEM)
    return pl.pallas_call(
        local_kernel,
        out_shape=jax.ShapeDtypeStruct((2, DEVICES // 2, PIECE, ANG), BF16),
        in_specs=[smem, smem, pl.BlockSpec(memory_space=pl.ANY), vmem, vmem, vmem, vmem],
        out_specs=vmem,
        scratch_shapes=[
            pltpu.VMEM((DEVICES * 8, ANG), F32),
            pltpu.VMEM((2, 1024, 1024), BF16),
            pltpu.VMEM((8, 1024, ANG), F32),
            pltpu.VMEM((BOX // 2 * parts, ANG), F32),
            pltpu.VMEM((parts, BOX * BOX), BF16),
            pltpu.VMEM((2, BOX * BOX, 2 * ANG), BF16),
            pltpu.VMEM((CPAD * RAD, ANG), F32),
            pltpu.VMEM((NROWS, cells), BF16),
            pltpu.VMEM((NROWS, ANG), F32),
            pltpu.VMEM((QROT * parts, cells), BF16),
            pltpu.VMEM((NROWS, QROT * parts), F32),
            pltpu.VMEM((NROWS, QROT * parts), BF16),
            pltpu.VMEM((NROWS, ANG), F32),
            pltpu.SemaphoreType.DMA((2,)),
        ],
        compiler_params=pltpu.CompilerParams(vmem_limit_bytes=60 * 1024 * 1024),
        name="local_terms",
    )(positions, counts, micrographs, dest_rows.reshape(1, parts), jnp.asarray(ys), jnp.asarray(xs), templates)


def remote(src, dst, send_sem, recv_sem, device):
    return pltpu.make_async_remote_copy(
        src_ref=src,
        dst_ref=dst,
        send_sem=send_sem,
        recv_sem=recv_sem,
        device_id=(device,),
        device_id_type=pl.DeviceIdType.MESH,
    )


def combine_kernel(packed, means, loglik, own, half, send, landed, gathered, crossed,
                   own_sem, half_send, half_recv, put_send, put_recv, get_send, get_recv, cross_send, cross_recv):
    me = lax.axis_index("dev")
    core = lax.rem(me, 2)
    chip = me // 2
    partner = me + 1 - 2 * core
    chunk = CHIPS // 4

    local = pltpu.make_async_copy(packed.at[core], own, own_sem)
    local.start()

    barrier = pltpu.get_barrier_semaphore()
    pl.semaphore_signal(barrier, inc=1, device_id=(partner,), device_id_type=pl.DeviceIdType.MESH)

    def greet(k, _):
        pl.semaphore_signal(
            barrier, inc=1, device_id=(2 * (chip ^ k) + core,), device_id_type=pl.DeviceIdType.MESH
        )
        return 0

    lax.fori_loop(1, CHIPS, greet, 0)
    pl.semaphore_wait(barrier, CHIPS)

    def half_copy(b):
        at = pl.ds((chip // chunk ^ b) * chunk, chunk)
        return remote(packed.at[1 - core, at], half.at[at], half_send.at[b], half_recv.at[b], partner)

    for b in range(4):
        half_copy(b).start()
    local.wait()

    def put(c, device_chip):
        return remote(
            send.at[c], landed.at[device_chip], put_send.at[c], put_recv.at[device_chip], 2 * c + core
        )

    for b in range(4):
        half_copy(b).wait_recv()

        def give(k, _, b=b):
            c = (chip // chunk ^ b) * chunk + (lax.rem(chip, chunk) ^ k)
            send[c] = (own[c].astype(F32) + half[c].astype(F32)).astype(BF16)

            @pl.when(c != chip)
            def _():
                put(c, chip).start()

            return 0

        lax.fori_loop(0, chunk, give, 0)

    def take(k, acc):
        c = chip ^ k
        remote(send.at[c], landed.at[c], put_send.at[c], put_recv.at[c], 2 * c + core).wait_recv()
        return acc + landed[c].astype(F32)

    acc = lax.fori_loop(1, CHIPS, take, send[chip].astype(F32))

    quarter = 2 * lax.rem(chip, 2) + core
    row = lax.broadcasted_iota(jnp.int32, (PIECE, ANG), 0)
    lane = lax.broadcasted_iota(jnp.int32, (PIECE, ANG), 1)
    which = jnp.where(row < 24, 24 * quarter + row, 96 + quarter)
    total = acc[25:26] + acc[26:27] + acc[30:31] + acc[31:32]
    total = jnp.sum(jnp.where(lane == which, total, 0.0), axis=1, keepdims=True)
    gathered[chip] = (acc / jnp.maximum(total, 1.0)).astype(BF16)
    loglik[...] = acc[27:28] + acc[28:29] + acc[29:30]

    def share(c, to):
        return remote(gathered.at[c], gathered.at[c], get_send.at[to], get_recv.at[c], 2 * to + core)

    def pass_on(c):
        return remote(gathered.at[c], crossed.at[c], cross_send.at[c], cross_recv.at[c], partner)

    def spread(k, _):
        share(chip, chip ^ k).start()
        return 0

    lax.fori_loop(1, CHIPS, spread, 0)
    pass_on(chip).start()

    def write(piece, c, k):
        r = c // 2
        q = 2 * lax.rem(c, 2) + k
        wide = piece.astype(F32)
        means[pl.ds(24 * RAD * q + r, 24, stride=RAD), :] = wide[:24]
        means[pl.ds((96 + q) * RAD + r, 1), :] = wide[24:25]

    write(gathered[chip], chip, core)

    def collect(k, _):
        c = chip ^ k
        share(c, c).wait_recv()
        pass_on(c).start()
        write(gathered[c], c, core)
        return 0

    lax.fori_loop(1, CHIPS, collect, 0)

    def cross(k, _):
        c = chip ^ k
        pass_on(c).wait_recv()
        write(crossed[c], c, 1 - core)
        return 0

    lax.fori_loop(0, CHIPS, cross, 0)

    for b in range(4):
        half_copy(b).wait_send()

    def drain(k, _):
        c = chip ^ k
        put(c, chip).wait_send()
        share(chip, c).wait_send()
        pass_on(c).wait_send()
        return 0

    lax.fori_loop(1, CHIPS, drain, 0)
    pass_on(chip).wait_send()


def combine(packed):
    block = pltpu.VMEM((CHIPS, PIECE, ANG), BF16)
    many = pltpu.SemaphoreType.DMA((CHIPS,))
    vmem = pl.BlockSpec(memory_space=pltpu.VMEM)
    return pl.pallas_call(
        combine_kernel,
        out_shape=(
            jax.ShapeDtypeStruct((CLASSES * RAD, ANG), F32),
            jax.ShapeDtypeStruct((1, ANG), F32),
        ),
        in_specs=[pl.BlockSpec(memory_space=pl.ANY)],
        out_specs=(vmem, vmem),
        scratch_shapes=[block] * 6
        + [pltpu.SemaphoreType.DMA, pltpu.SemaphoreType.DMA((4,)), pltpu.SemaphoreType.DMA((4,))]
        + [many] * 6,
        compiler_params=pltpu.CompilerParams(collective_id=0, has_side_effects=True),
        name="combine",
    )(packed)


def on_device(micrographs, positions, counts, dest_rows, templates):
    packed = local_terms(micrographs, positions, counts, dest_rows, templates)
    means, loglik = combine(packed)
    return means.reshape(CLASSES, RAD, ANG), loglik.reshape(ANG)


def solution(mesh):
    P = jax.sharding.PartitionSpec
    return jax.shard_map(
        on_device,
        mesh=mesh,
        in_specs=(P("dev", None, None), P(None, "dev", None), P("dev"), P("dev", None), P()),
        out_specs=(P(), P("dev")),
        check_vma=False,
    )
```

```python
import functools
import numpy as np
import jax
import jax.numpy as jnp
from jax import lax
from jax.experimental import pallas as pl
from jax.experimental.pallas import tpu as pltpu

BOX = 64
RAD = 32
ANG = 128
CLASSES = 100
ROTS = 36
CPAD = 104
QROT = 4
BASE = 9
NROWS = 4 * 2 * CPAD + 112
DEVICES = 128
CHIPS = DEVICES // 2
PIECE = 32
F32 = jnp.float32
BF16 = jnp.bfloat16


def sample_points():
    center = np.float32((BOX - 1) / 2.0)
    radius = (np.arange(RAD, dtype=np.float32) + np.float32(0.5)) * np.float32(BOX / 2.0 - 1.0) / np.float32(RAD)
    theta = np.float32(2.0 * np.pi) * np.arange(ANG, dtype=np.float32) / np.float32(ANG)
    ys = (center + radius[:, None] * np.sin(theta)[None, :]).reshape(1, -1)
    xs = (center + radius[:, None] * np.cos(theta)[None, :]).reshape(1, -1)
    def ordered(v):
        v = v.astype(np.float32).reshape(RAD // 4, 2, 2, 2, ANG // 2)
        v = v.transpose(0, 3, 1, 2, 4)
        v = np.stack([v[:, 0], v[:, 1, :, ::-1]], axis=1)
        return v.reshape(1, -1)

    return ordered(ys), ordered(xs)


def rotation_taps():
    a = np.arange(ANG, dtype=np.float32)
    taps = []
    for k in range(BASE):
        shift = np.float32(k) * np.float32(ANG) / np.float32(ROTS)
        d = a - np.float32(0) - shift
        d = d - ANG * np.floor(d / np.float32(ANG) + np.float32(0.5))
        w = np.maximum(np.float32(0), np.float32(1) - np.abs(d)).astype(jnp.bfloat16).astype(np.float32)
        first = int(32 * k // 9)
        taps.append((first, float(w[first]), float(w[(first + 1) % ANG]) if k else 0.0))
    return taps


TAPS = rotation_taps()


def turned_rows(x, i):
    if i == 8:
        return x[8 * CPAD : 9 * CPAD]
    pair = x[(i // 2) * 2 * CPAD : (i // 2 + 1) * 2 * CPAD].reshape(CPAD // 8, 16, x.shape[1])
    return pair[:, 8 * (i % 2) : 8 * (i % 2) + 8].reshape(CPAD, x.shape[1])


def local_kernel(pos, counts, mic, dest, ys, xs, tmpl, out, extra, raw, planes, flat, boxes, wtile, tflat, rot, esum, shifted, scores, weights, tsum, sums_a, sums_b, sems):
    mics = mic.shape[0]
    slots = pos.shape[2]
    parts = mics * slots

    def fetch(i):
        return pltpu.make_async_copy(mic.at[i], raw.at[i % 2], sems.at[i % 2])

    fetch(0).start()
    fetch(1).start()

    lane1 = lax.broadcasted_iota(jnp.int32, (1, ANG), 1)

    tflat[pl.ds(CLASSES * RAD, 12 * RAD), :] = jnp.zeros((12 * RAD, ANG), F32)
    tflat[pl.ds(0, CLASSES * RAD), :] = tmpl[...].reshape(CLASSES * RAD, ANG).astype(F32)

    def rotate_tile(n, _):
        t = 6 - n
        starts = [pl.multiple_of(k * 2 * CPAD + (2 * t + h) * 16, 16) for k in range(4) for h in range(2)]
        starts.append(pl.multiple_of(8 * CPAD + t * 16, 16))

        def rotate_radius(r, sums):
            x = tflat[pl.ds(t * 16 * RAD + r, 16, stride=RAD), :]
            x1 = pltpu.roll(x, 1, 1)
            col = pl.ds(pl.multiple_of(r * ANG, ANG), ANG)
            turned = []
            for first, w0, w1 in TAPS:
                y = x if w1 == 0.0 else w0 * x + w1 * x1
                turned.append(pltpu.roll(y, first, 1) if first else y)
            tiles = [
                jnp.concatenate([turned[2 * k][8 * h : 8 * h + 8], turned[2 * k + 1][8 * h : 8 * h + 8]], axis=0)
                for k in range(4)
                for h in range(2)
            ] + [turned[8]]
            new = []
            for start, tile, total in zip(starts, tiles, sums):
                tile = tile.astype(BF16)
                rot[pl.ds(start, 16), col] = tile
                wide = tile.astype(F32)
                new.append(total + wide * wide)
            return tuple(new)

        sums = lax.fori_loop(0, RAD, rotate_radius, (jnp.zeros((16, ANG), F32),) * 9, unroll=2)
        for start, total in zip(starts, sums):
            esum[pl.ds(start, 16), :] = total
        return 0

    lax.fori_loop(0, 7, rotate_tile, 0)

    lanes = lax.broadcasted_iota(jnp.int32, (BOX // 2, ANG), 1)
    for i in range(mics):
        fetch(i).wait()
        for t in range(8):
            planes[t, :, :] = raw[i % 2, :, t * ANG : (t + 1) * ANG].astype(F32)
        if i + 2 < mics:
            fetch(i + 2).start()

        def cut(j, _, i=i):
            y = pos[0, i, j]
            x = pos[1, i, j]
            t = x >> 7
            s = x & 127
            t1 = jnp.minimum(t + 1, 7)
            even = pl.ds(y, BOX // 2, stride=2)
            odd = pl.ds(y + 1, BOX // 2, stride=2)
            keep = lanes >= s
            e = jnp.where(keep, planes[t, even, :], planes[t1, even, :])
            o = jnp.where(keep, planes[t, odd, :], planes[t1, odd, :])
            e = pltpu.roll(e, (ANG - s) & 127, 1)
            o = pltpu.roll(o, (ANG + BOX - s) & 127, 1)
            flat[pl.ds(i * slots + j, BOX // 2, stride=parts), :] = jnp.where(lanes < BOX, e, o)
            return 0

        lax.fori_loop(0, slots, cut, 0, unroll=8)

    for s in range(BOX // 2):
        boxes[:, s * ANG : (s + 1) * ANG] = flat[pl.ds(s * parts, parts), :].astype(BF16)

    pix = lax.broadcasted_iota(jnp.int32, (BOX, 2 * ANG), 0).astype(F32)
    left = lax.broadcasted_iota(jnp.int32, (parts, ANG), 1) < BOX
    for g in range(RAD // 4):
        radius = (4 * g + 3.5) * (BOX / 2.0 - 1.0) / RAD
        reach = (int(np.floor(31.501 + radius)) + 3) // 2 * 2
        halves = []
        for side in range(2):
            low, high = (30, reach) if side == 0 else (BOX - reach, 34)
            cols = slice((2 * g + side) * 2 * ANG, (2 * g + side + 1) * 2 * ANG)
            rw = jnp.maximum(0.0, 1.0 - jnp.abs(pix - ys[:, cols]))
            cw = jnp.maximum(0.0, 1.0 - jnp.abs(pix - xs[:, cols]))
            w = wtile.at[side]
            for u in range(low, high):
                w[(u - low) * BOX : (u - low + 1) * BOX, :] = (rw[u : u + 1, :] * cw).astype(BF16)
            halves.append(
                jnp.dot(
                    boxes[:, low * BOX : high * BOX],
                    w[: (high - low) * BOX, :],
                    preferred_element_type=F32,
                )
            )
        for m in range(2):
            upper = halves[0][:, m * ANG : (m + 1) * ANG]
            lower = halves[1][:, m * ANG : (m + 1) * ANG]
            for h in range(2):
                whole = jnp.where(left, upper, lower) if h == 0 else jnp.where(left, lower, upper)
                c0 = (4 * g + 2 * m + h) * ANG
                for j in range(QROT):
                    turn = (BOX * h - 32 * j) % ANG
                    part = pltpu.roll(whole, turn, 1) if turn else whole
                    shifted[j * parts : (j + 1) * parts, c0 : c0 + ANG] = part.astype(BF16)

    rows = lax.broadcasted_iota(jnp.int32, (NROWS, 1), 0)
    energy = 0.5 * jnp.sum(esum[...], axis=1, keepdims=True)
    paired = lax.rem(rows >> 4, 13) * 8 + (rows & 7)
    pad = jnp.where(rows < 8 * CPAD, paired, rows - 8 * CPAD) >= CLASSES
    energy = jnp.where(pad, 1e30, energy)

    def score(j, peak):
        rows_j = pl.ds(pl.multiple_of(j * parts, parts), parts)
        prod = lax.dot_general(rot[...], shifted[rows_j, :], (((1,), (1,)), ((), ())), preferred_element_type=F32)
        prod = prod - energy
        scores[:, rows_j] = prod
        return jnp.maximum(peak, jnp.max(prod, axis=0, keepdims=True))

    peak = lax.fori_loop(0, QROT, score, jnp.full((1, parts), -3e38, F32))
    peak4 = jnp.concatenate([peak] * QROT, axis=1)

    def expo(n, acc):
        rr = pl.ds(pl.multiple_of(n * 16, 16), 16)
        e = jnp.exp(scores[rr, :] - peak4)
        scores[rr, :] = e
        return acc + e[:8] + e[8:]

    acc = lax.fori_loop(0, NROWS // 16, expo, jnp.zeros((8, QROT * parts), F32))
    norm = jnp.sum(acc, axis=0, keepdims=True)
    norm = sum(norm[:, j * parts : (j + 1) * parts] for j in range(QROT))
    loglik = peak + jnp.log(norm)

    lane = lax.broadcasted_iota(jnp.int32, (1, parts), 1)
    target = jnp.concatenate([dest[i : i + 1, :] for i in range(mics)], axis=1)
    live = target >= 0
    for i in range(mics):
        live = live & ((lane < i * slots + counts[i]) | (lane >= (i + 1) * slots))
    inv = jnp.where(live, 1.0 / norm, 0.0)
    inv4 = jnp.concatenate([inv] * QROT, axis=1)

    def weigh(n, _):
        rr = pl.ds(pl.multiple_of(n * 16, 16), 16)
        w = (scores[rr, :] * inv4).astype(BF16)
        weights[rr, :] = w
        wide = w.astype(F32)
        tsum[rr, :] = sum(wide[:, k * ANG : (k + 1) * ANG] for k in range(QROT * parts // ANG))
        return 0

    lax.fori_loop(0, NROWS // 16, weigh, 0)
    tot = jnp.sum(sum(turned_rows(tsum[...], i) for i in range(BASE)), axis=1, keepdims=True)
    spot = lax.broadcasted_iota(jnp.int32, (CPAD, ANG), 0) == lax.broadcasted_iota(jnp.int32, (CPAD, ANG), 1)
    tot = jnp.sum(jnp.where(spot, tot, 0.0), axis=0, keepdims=True)
    high = tot.astype(BF16).astype(F32)
    first = lax.rem(lax.axis_index("dev"), 2) == 0
    extra[...] = jnp.zeros_like(extra)
    for value, here, there in ((high, 1, 6), (tot - high, 2, 7)):
        value = jnp.broadcast_to(value, (DEVICES, ANG))
        extra[pl.ds(here, DEVICES, stride=8), :] = jnp.where(first, value, 0.0)
        extra[pl.ds(there, DEVICES, stride=8), :] = jnp.where(first, 0.0, value)

    which = lax.broadcasted_iota(jnp.int32, (ANG, parts), 0)
    owner = jnp.where((which == (target >> 7)) & live, 1.0, 0.0)
    row = jnp.where(which == (target & 127), 1.0, 0.0).astype(BF16)
    rest = loglik
    for k in range(3):
        piece = rest.astype(BF16).astype(F32)
        table = lax.dot_general((owner * piece).astype(BF16), row, (((1,), (1,)), ((), ())), preferred_element_type=F32)
        extra[pl.ds(3 + k, DEVICES, stride=8), :] = table
        rest = rest - piece

    top = lax.broadcasted_iota(jnp.int32, (8, ANG), 0)

    def product(g, into):
        cols = pl.ds(pl.multiple_of(g * 2 * ANG, 2 * ANG), 2 * ANG)
        into[...] = jnp.dot(weights[...], shifted[:, cols], preferred_element_type=F32)

    def fold(g, source):
        for k in range(2):
            sum0 = jnp.zeros((CPAD, ANG), F32)
            sum1 = jnp.zeros((CPAD, ANG), F32)
            half = source[:, k * ANG : (k + 1) * ANG]
            for i, (first, w0, w1) in enumerate(TAPS):
                q = turned_rows(half, i)
                if first:
                    q = pltpu.roll(q, ANG - first, 1)
                sum0 += w0 * q
                if w1:
                    sum1 += w1 * q
            total = sum0 + pltpu.roll(sum1, ANG - 1, 1)
            r = 2 * g + k
            for q in range(4):
                tail = total[96:] if q == 0 else pltpu.roll(total[96:], 8 - q, 0)
                spare = extra[pl.ds(pl.multiple_of((4 * r + q) * 8, 8), 8), :]
                tail = jnp.where(top == 0, tail, spare)
                piece = jnp.concatenate([total[24 * q : 24 * q + 24], tail], axis=0)
                out[q % 2, 2 * r + q // 2, :, :] = piece.astype(BF16)

    product(0, sums_a)

    def collect(n, _):
        product(2 * n + 1, sums_b)
        fold(2 * n, sums_a)
        product(2 * n + 2, sums_a)
        fold(2 * n + 1, sums_b)
        return 0

    lax.fori_loop(0, RAD // 4 - 1, collect, 0)
    product(RAD // 2 - 1, sums_b)
    fold(RAD // 2 - 2, sums_a)
    fold(RAD // 2 - 1, sums_b)


def local_terms(micrographs, positions, counts, dest_rows, templates):
    mics, slots = dest_rows.shape
    parts = mics * slots
    cells = RAD * ANG
    ys, xs = sample_points()
    vmem = pl.BlockSpec(memory_space=pltpu.VMEM)
    smem = pl.BlockSpec(memory_space=pltpu.SMEM)
    return pl.pallas_call(
        local_kernel,
        out_shape=jax.ShapeDtypeStruct((2, DEVICES // 2, PIECE, ANG), BF16),
        in_specs=[smem, smem, pl.BlockSpec(memory_space=pl.ANY), vmem, vmem, vmem, vmem],
        out_specs=vmem,
        scratch_shapes=[
            pltpu.VMEM((DEVICES * 8, ANG), F32),
            pltpu.VMEM((2, 1024, 1024), BF16),
            pltpu.VMEM((8, 1024, ANG), F32),
            pltpu.VMEM((BOX // 2 * parts, ANG), F32),
            pltpu.VMEM((parts, BOX * BOX), BF16),
            pltpu.VMEM((2, 34 * BOX, 2 * ANG), BF16),
            pltpu.VMEM((112 * RAD, ANG), F32),
            pltpu.VMEM((NROWS, cells), BF16),
            pltpu.VMEM((NROWS, ANG), F32),
            pltpu.VMEM((QROT * parts, cells), BF16),
            pltpu.VMEM((NROWS, QROT * parts), F32),
            pltpu.VMEM((NROWS, QROT * parts), BF16),
            pltpu.VMEM((NROWS, ANG), F32),
            pltpu.VMEM((NROWS, 2 * ANG), F32),
            pltpu.VMEM((NROWS, 2 * ANG), F32),
            pltpu.SemaphoreType.DMA((2,)),
        ],
        compiler_params=pltpu.CompilerParams(vmem_limit_bytes=60 * 1024 * 1024),
        name="local_terms",
    )(positions, counts, micrographs, dest_rows, jnp.asarray(ys), jnp.asarray(xs), templates)


def remote(src, dst, send_sem, recv_sem, device):
    return pltpu.make_async_remote_copy(
        src_ref=src,
        dst_ref=dst,
        send_sem=send_sem,
        recv_sem=recv_sem,
        device_id=(device,),
        device_id_type=pl.DeviceIdType.MESH,
    )


def combine_kernel(packed, means, loglik, own, half, send, landed, gathered, crossed,
                   own_sem, half_send, half_recv, put_send, put_recv, get_send, get_recv, cross_send, cross_recv):
    me = lax.axis_index("dev")
    core = lax.rem(me, 2)
    chip = me // 2
    partner = me + 1 - 2 * core
    chunk = CHIPS // 4

    local = pltpu.make_async_copy(packed.at[core], own, own_sem)
    local.start()

    barrier = pltpu.get_barrier_semaphore()
    pl.semaphore_signal(barrier, inc=1, device_id=(partner,), device_id_type=pl.DeviceIdType.MESH)

    def greet(k, _):
        pl.semaphore_signal(
            barrier, inc=1, device_id=(2 * (chip ^ k) + core,), device_id_type=pl.DeviceIdType.MESH
        )
        return 0

    lax.fori_loop(1, CHIPS, greet, 0)
    pl.semaphore_wait(barrier, CHIPS)

    def half_copy(b):
        at = pl.ds((chip // chunk ^ b) * chunk, chunk)
        return remote(packed.at[1 - core, at], half.at[at], half_send.at[b], half_recv.at[b], partner)

    for b in range(4):
        half_copy(b).start()
    local.wait()

    def put(c, device_chip):
        return remote(
            send.at[c], landed.at[device_chip], put_send.at[c], put_recv.at[device_chip], 2 * c + core
        )

    for b in range(4):
        half_copy(b).wait_recv()

        def give(k, _, b=b):
            c = (chip // chunk ^ b) * chunk + (lax.rem(chip, chunk) ^ k)
            send[c] = (own[c].astype(F32) + half[c].astype(F32)).astype(BF16)

            @pl.when(c != chip)
            def _():
                put(c, chip).start()

            return 0

        lax.fori_loop(0, chunk, give, 0)

    def take(k, acc):
        c = chip ^ k
        remote(send.at[c], landed.at[c], put_send.at[c], put_recv.at[c], 2 * c + core).wait_recv()
        return acc + landed[c].astype(F32)

    acc = lax.fori_loop(1, CHIPS, take, send[chip].astype(F32))

    quarter = 2 * lax.rem(chip, 2) + core
    row = lax.broadcasted_iota(jnp.int32, (PIECE, ANG), 0)
    lane = lax.broadcasted_iota(jnp.int32, (PIECE, ANG), 1)
    which = jnp.where(row < 24, 24 * quarter + row, 96 + quarter)
    total = acc[25:26] + acc[26:27] + acc[30:31] + acc[31:32]
    total = jnp.sum(jnp.where(lane == which, total, 0.0), axis=1, keepdims=True)
    gathered[chip] = (acc / jnp.maximum(total, 1.0)).astype(BF16)
    loglik[...] = acc[27:28] + acc[28:29] + acc[29:30]

    def share(c, to):
        return remote(gathered.at[c], gathered.at[c], get_send.at[to], get_recv.at[c], 2 * to + core)

    def pass_on(c):
        return remote(gathered.at[c], crossed.at[c], cross_send.at[c], cross_recv.at[c], partner)

    def spread(k, _):
        share(chip, chip ^ k).start()
        return 0

    lax.fori_loop(1, CHIPS, spread, 0)
    pass_on(chip).start()

    def write(piece, c, k):
        r = c // 2
        q = 2 * lax.rem(c, 2) + k
        wide = piece.astype(F32)
        means[pl.ds(24 * RAD * q + r, 24, stride=RAD), :] = wide[:24]
        means[pl.ds((96 + q) * RAD + r, 1), :] = wide[24:25]

    write(gathered[chip], chip, core)

    def collect(k, _):
        c = chip ^ k
        share(c, c).wait_recv()
        pass_on(c).start()
        write(gathered[c], c, core)
        return 0

    lax.fori_loop(1, CHIPS, collect, 0)

    def cross(k, _):
        c = chip ^ k
        pass_on(c).wait_recv()
        write(crossed[c], c, 1 - core)
        return 0

    lax.fori_loop(0, CHIPS, cross, 0)

    for b in range(4):
        half_copy(b).wait_send()

    def drain(k, _):
        c = chip ^ k
        put(c, chip).wait_send()
        share(chip, c).wait_send()
        pass_on(c).wait_send()
        return 0

    lax.fori_loop(1, CHIPS, drain, 0)
    pass_on(chip).wait_send()


def combine(packed):
    block = pltpu.VMEM((CHIPS, PIECE, ANG), BF16)
    many = pltpu.SemaphoreType.DMA((CHIPS,))
    vmem = pl.BlockSpec(memory_space=pltpu.VMEM)
    return pl.pallas_call(
        combine_kernel,
        out_shape=(
            jax.ShapeDtypeStruct((CLASSES * RAD, ANG), F32),
            jax.ShapeDtypeStruct((1, ANG), F32),
        ),
        in_specs=[pl.BlockSpec(memory_space=pl.ANY)],
        out_specs=(vmem, vmem),
        scratch_shapes=[block] * 6
        + [pltpu.SemaphoreType.DMA, pltpu.SemaphoreType.DMA((4,)), pltpu.SemaphoreType.DMA((4,))]
        + [many] * 6,
        compiler_params=pltpu.CompilerParams(collective_id=0, has_side_effects=True),
        name="combine",
    )(packed)


def on_device(micrographs, positions, counts, dest_rows, templates):
    packed = local_terms(micrographs, positions, counts, dest_rows, templates)
    means, loglik = combine(packed)
    return means.reshape(CLASSES, RAD, ANG), loglik.reshape(ANG)


def solution(mesh):
    P = jax.sharding.PartitionSpec
    return jax.shard_map(
        on_device,
        mesh=mesh,
        in_specs=(P("dev", None, None), P(None, "dev", None), P("dev"), P("dev", None), P()),
        out_specs=(P(), P("dev")),
        check_vma=False,
    )
```

```python
import functools
import numpy as np
import jax
import jax.numpy as jnp
from jax import lax
from jax.experimental import pallas as pl
from jax.experimental.pallas import tpu as pltpu

BOX = 64
RAD = 32
ANG = 128
CLASSES = 100
ROTS = 36
CPAD = 104
QROT = 4
BASE = 9
NROWS = 4 * 2 * CPAD + 112
DEVICES = 128
CHIPS = DEVICES // 2
PIECE = 32
F32 = jnp.float32
BF16 = jnp.bfloat16


def sample_points():
    center = np.float32((BOX - 1) / 2.0)
    radius = (np.arange(RAD, dtype=np.float32) + np.float32(0.5)) * np.float32(BOX / 2.0 - 1.0) / np.float32(RAD)
    theta = np.float32(2.0 * np.pi) * np.arange(ANG, dtype=np.float32) / np.float32(ANG)
    ys = (center + radius[:, None] * np.sin(theta)[None, :]).reshape(1, -1)
    xs = (center + radius[:, None] * np.cos(theta)[None, :]).reshape(1, -1)
    def ordered(v):
        v = v.astype(np.float32).reshape(RAD // 4, 2, 2, 2, ANG // 2)
        v = v.transpose(0, 3, 1, 2, 4)
        v = np.stack([v[:, 0], v[:, 1, :, ::-1]], axis=1)
        return v.reshape(1, -1)

    return ordered(ys), ordered(xs)


def rotation_taps():
    a = np.arange(ANG, dtype=np.float32)
    taps = []
    for k in range(BASE):
        shift = np.float32(k) * np.float32(ANG) / np.float32(ROTS)
        d = a - np.float32(0) - shift
        d = d - ANG * np.floor(d / np.float32(ANG) + np.float32(0.5))
        w = np.maximum(np.float32(0), np.float32(1) - np.abs(d)).astype(jnp.bfloat16).astype(np.float32)
        first = int(32 * k // 9)
        taps.append((first, float(w[first]), float(w[(first + 1) % ANG]) if k else 0.0))
    return taps


TAPS = rotation_taps()


def turned_rows(x, i):
    if i == 8:
        return x[8 * CPAD : 9 * CPAD]
    pair = x[(i // 2) * 2 * CPAD : (i // 2 + 1) * 2 * CPAD].reshape(CPAD // 8, 16, x.shape[1])
    return pair[:, 8 * (i % 2) : 8 * (i % 2) + 8].reshape(CPAD, x.shape[1])


def remote(src, dst, send_sem, recv_sem, device):
    return pltpu.make_async_remote_copy(
        src_ref=src,
        dst_ref=dst,
        send_sem=send_sem,
        recv_sem=recv_sem,
        device_id=(device,),
        device_id_type=pl.DeviceIdType.MESH,
    )


def iteration_kernel(pos, counts, mic, dest, ys, xs, tmpl, means, evidence, extra, raw, planes, flat, boxes, wtile, tflat, byrad, rmat, rot, esum, shifted, scores, weights, tsum, sums_a, sums_b, out, half, send, landed, gathered, crossed, sems,
                     half_send, half_recv, put_send, put_recv, get_send, get_recv, cross_send, cross_recv):
    mics = mic.shape[0]
    slots = pos.shape[2]
    parts = mics * slots

    me = lax.axis_index("dev")
    core = lax.rem(me, 2)
    chip = me // 2
    partner = me + 1 - 2 * core

    barrier = pltpu.get_barrier_semaphore()
    pl.semaphore_signal(barrier, inc=1, device_id=(partner,), device_id_type=pl.DeviceIdType.MESH)

    def greet(k, _):
        pl.semaphore_signal(
            barrier, inc=1, device_id=(2 * (chip ^ k) + core,), device_id_type=pl.DeviceIdType.MESH
        )
        return 0

    lax.fori_loop(1, CHIPS, greet, 0)

    def fetch(i):
        return pltpu.make_async_copy(mic.at[i], raw.at[i % 2], sems.at[i % 2])

    fetch(0).start()
    fetch(1).start()

    lane1 = lax.broadcasted_iota(jnp.int32, (1, ANG), 1)

    away = lax.broadcasted_iota(jnp.int32, (ANG, ANG), 1) - lax.broadcasted_iota(jnp.int32, (ANG, ANG), 0)
    for i, (first, w0, w1) in enumerate(TAPS):
        step = (away - first) & 127
        turn = jnp.where(step == 0, w0, jnp.where(step == 1, w1, 0.0))
        rmat[:, i * ANG : (i + 1) * ANG] = turn.astype(BF16)
    tflat[pl.ds(CLASSES * RAD, (CPAD - CLASSES) * RAD), :] = jnp.zeros(((CPAD - CLASSES) * RAD, ANG), F32)
    tflat[pl.ds(0, CLASSES * RAD), :] = tmpl[...].reshape(CLASSES * RAD, ANG).astype(F32)
    esum[...] = jnp.zeros_like(esum)
    tiles = CPAD // 8

    def regroup(n, _):
        pair = [tflat[pl.ds(2 * n + h, CPAD, stride=RAD), :] for h in range(2)]
        byrad[pl.ds(pl.multiple_of(n * 2 * CPAD, 16), 2 * CPAD), :] = jnp.concatenate(pair, axis=0).astype(BF16)
        return 0

    lax.fori_loop(0, RAD // 2, regroup, 0, unroll=2)

    def rotate_block(n, _):
        few = 4
        block = byrad[pl.ds(pl.multiple_of(n * few * CPAD, 16), few * CPAD), :]
        for k in range(5):
            start, height = (k * 2 * CPAD, 2 * CPAD) if k < 4 else (8 * CPAD, 112)
            wide = jnp.dot(block, rmat[:, k * 2 * ANG : min(k * 2 + 2, 9) * ANG], preferred_element_type=F32)
            total = jnp.zeros((height, ANG), F32)
            for h in range(few):
                some = wide[h * CPAD : (h + 1) * CPAD]
                if k < 4:
                    some = [some[:, m * ANG : (m + 1) * ANG].reshape(tiles, 8, ANG) for m in range(2)]
                    some = jnp.concatenate(some, axis=1).reshape(2 * CPAD, ANG)
                else:
                    some = jnp.concatenate([some, jnp.zeros((8, ANG), F32)], axis=0)
                some = some.astype(BF16)
                col = pl.ds(pl.multiple_of((n * few + h) * ANG, ANG), ANG)
                rot[start : start + height, col] = some
                some = some.astype(F32)
                total += some * some
            esum[start : start + height, :] += total
        return 0

    lax.fori_loop(0, RAD // 4, rotate_block, 0)

    lanes = lax.broadcasted_iota(jnp.int32, (BOX // 2, ANG), 1)
    for i in range(mics):
        fetch(i).wait()
        for t in range(8):
            planes[t, :, :] = raw[i % 2, :, t * ANG : (t + 1) * ANG].astype(F32)
        if i + 2 < mics:
            fetch(i + 2).start()

        def cut(j, _, i=i):
            y = pos[0, i, j]
            x = pos[1, i, j]
            t = x >> 7
            s = x & 127
            t1 = jnp.minimum(t + 1, 7)
            even = pl.ds(y, BOX // 2, stride=2)
            odd = pl.ds(y + 1, BOX // 2, stride=2)
            keep = lanes >= s
            e = jnp.where(keep, planes[t, even, :], planes[t1, even, :])
            o = jnp.where(keep, planes[t, odd, :], planes[t1, odd, :])
            e = pltpu.roll(e, (ANG - s) & 127, 1)
            o = pltpu.roll(o, (ANG + BOX - s) & 127, 1)
            flat[pl.ds(pl.multiple_of((i * slots + j) * (BOX // 2), BOX // 2), BOX // 2), :] = jnp.where(lanes < BOX, e, o)
            return 0

        lax.fori_loop(0, slots, cut, 0, unroll=8)

    for s in range(BOX // 2):
        boxes[:, s * ANG : (s + 1) * ANG] = flat[pl.ds(s, parts, stride=BOX // 2), :].astype(BF16)

    pix = lax.broadcasted_iota(jnp.int32, (BOX, 2 * ANG), 0).astype(F32)
    left = lax.broadcasted_iota(jnp.int32, (parts, ANG), 1) < BOX
    for g in range(RAD // 4):
        radius = (4 * g + 3.5) * (BOX / 2.0 - 1.0) / RAD
        reach = (int(np.floor(31.501 + radius)) + 3) // 2 * 2
        halves = []
        for side in range(2):
            low, high = (30, reach) if side == 0 else (BOX - reach, 34)
            cols = slice((2 * g + side) * 2 * ANG, (2 * g + side + 1) * 2 * ANG)
            rw = jnp.maximum(0.0, 1.0 - jnp.abs(pix - ys[:, cols]))
            cw = jnp.maximum(0.0, 1.0 - jnp.abs(pix - xs[:, cols]))
            w = wtile.at[side]
            for u in range(low, high):
                w[(u - low) * BOX : (u - low + 1) * BOX, :] = (rw[u : u + 1, :] * cw).astype(BF16)
            halves.append(
                jnp.dot(
                    boxes[:, low * BOX : high * BOX],
                    w[: (high - low) * BOX, :],
                    preferred_element_type=F32,
                )
            )
        for m in range(2):
            upper = halves[0][:, m * ANG : (m + 1) * ANG]
            lower = halves[1][:, m * ANG : (m + 1) * ANG]
            for h in range(2):
                whole = jnp.where(left, upper, lower) if h == 0 else jnp.where(left, lower, upper)
                c0 = (4 * g + 2 * m + h) * ANG
                for j in range(QROT):
                    turn = (BOX * h - 32 * j) % ANG
                    part = pltpu.roll(whole, turn, 1) if turn else whole
                    shifted[j * parts : (j + 1) * parts, c0 : c0 + ANG] = part.astype(BF16)

    rows = lax.broadcasted_iota(jnp.int32, (NROWS, 1), 0)
    energy = 0.5 * jnp.sum(esum[...], axis=1, keepdims=True)
    paired = lax.rem(rows >> 4, 13) * 8 + (rows & 7)
    pad = jnp.where(rows < 8 * CPAD, paired, rows - 8 * CPAD) >= CLASSES
    energy = jnp.where(pad, 1e30, energy)

    def score(j, peak):
        rows_j = pl.ds(pl.multiple_of(j * parts, parts), parts)
        prod = lax.dot_general(rot[...], shifted[rows_j, :], (((1,), (1,)), ((), ())), preferred_element_type=F32)
        prod = prod - energy
        scores[:, rows_j] = prod
        return jnp.maximum(peak, jnp.max(prod, axis=0, keepdims=True))

    peak = lax.fori_loop(0, QROT, score, jnp.full((1, parts), -3e38, F32))
    peak4 = jnp.concatenate([peak] * QROT, axis=1)

    def expo(n, acc):
        rr = pl.ds(pl.multiple_of(n * 16, 16), 16)
        e = jnp.exp(scores[rr, :] - peak4)
        scores[rr, :] = e
        return acc + e[:8] + e[8:]

    acc = lax.fori_loop(0, NROWS // 16, expo, jnp.zeros((8, QROT * parts), F32))
    norm = jnp.sum(acc, axis=0, keepdims=True)
    norm = sum(norm[:, j * parts : (j + 1) * parts] for j in range(QROT))
    loglik = peak + jnp.log(norm)

    lane = lax.broadcasted_iota(jnp.int32, (1, parts), 1)
    target = jnp.concatenate([dest[i : i + 1, :] for i in range(mics)], axis=1)
    live = target >= 0
    for i in range(mics):
        live = live & ((lane < i * slots + counts[i]) | (lane >= (i + 1) * slots))
    inv = jnp.where(live, 1.0 / norm, 0.0)
    inv4 = jnp.concatenate([inv] * QROT, axis=1)

    def weigh(n, _):
        rr = pl.ds(pl.multiple_of(n * 16, 16), 16)
        w = (scores[rr, :] * inv4).astype(BF16)
        weights[rr, :] = w
        wide = w.astype(F32)
        tsum[rr, :] = sum(wide[:, k * ANG : (k + 1) * ANG] for k in range(QROT * parts // ANG))
        return 0

    lax.fori_loop(0, NROWS // 16, weigh, 0)
    tot = jnp.sum(sum(turned_rows(tsum[...], i) for i in range(BASE)), axis=1, keepdims=True)
    spot = lax.broadcasted_iota(jnp.int32, (CPAD, ANG), 0) == lax.broadcasted_iota(jnp.int32, (CPAD, ANG), 1)
    tot = jnp.sum(jnp.where(spot, tot, 0.0), axis=0, keepdims=True)
    high = tot.astype(BF16).astype(F32)
    first = core == 0
    extra[...] = jnp.zeros_like(extra)
    for value, here, there in ((high, 1, 6), (tot - high, 2, 7)):
        value = jnp.broadcast_to(value, (DEVICES, ANG))
        extra[pl.ds(here, DEVICES, stride=8), :] = jnp.where(first, value, 0.0)
        extra[pl.ds(there, DEVICES, stride=8), :] = jnp.where(first, 0.0, value)

    which = lax.broadcasted_iota(jnp.int32, (ANG, parts), 0)
    owner = jnp.where((which == (target >> 7)) & live, 1.0, 0.0)
    row = jnp.where(which == (target & 127), 1.0, 0.0).astype(BF16)
    rest = loglik
    for k in range(3):
        piece = rest.astype(BF16).astype(F32)
        table = lax.dot_general((owner * piece).astype(BF16), row, (((1,), (1,)), ((), ())), preferred_element_type=F32)
        extra[pl.ds(3 + k, DEVICES, stride=8), :] = table
        rest = rest - piece

    top = lax.broadcasted_iota(jnp.int32, (8, ANG), 0)

    def turn(n):
        return n ^ (chip // 4)

    def product(n, into):
        g = turn(n)
        cols = pl.ds(pl.multiple_of(g * 2 * ANG, 2 * ANG), 2 * ANG)
        into[...] = jnp.dot(weights[...], shifted[:, cols], preferred_element_type=F32)

    def fold(n, source):
        g = turn(n)
        for k in range(2):
            sum0 = jnp.zeros((CPAD, ANG), F32)
            sum1 = jnp.zeros((CPAD, ANG), F32)
            half = source[:, k * ANG : (k + 1) * ANG]
            for i, (first, w0, w1) in enumerate(TAPS):
                q = turned_rows(half, i)
                if first:
                    q = pltpu.roll(q, ANG - first, 1)
                sum0 += w0 * q
                if w1:
                    sum1 += w1 * q
            total = sum0 + pltpu.roll(sum1, ANG - 1, 1)
            r = 2 * g + k
            for q in range(4):
                tail = total[96:] if q == 0 else pltpu.roll(total[96:], 8 - q, 0)
                spare = extra[pl.ds(pl.multiple_of((4 * r + q) * 8, 8), 8), :]
                tail = jnp.where(top == 0, tail, spare)
                piece = jnp.concatenate([total[24 * q : 24 * q + 24], tail], axis=0)
                out[q % 2, 2 * r + q // 2, :, :] = piece.astype(BF16)

    def half_copy(n):
        at = pl.ds(4 * turn(n), 4)
        return remote(out.at[1 - core, at], half.at[at], half_send.at[n], half_recv.at[n], partner)

    def put(c, slot):
        return remote(send.at[c], landed.at[slot], put_send.at[c], put_recv.at[slot], 2 * c + core)

    def give(n):
        half_copy(n).wait_recv()
        for m in range(4):
            c = 4 * turn(n) + m
            send[c] = (out[core, c].astype(F32) + half[c].astype(F32)).astype(BF16)
        for m in range(4):
            c = 4 * turn(n) + m

            @pl.when(c != chip)
            def _():
                put(c, chip).start()

    product(0, sums_a)
    pl.semaphore_wait(barrier, CHIPS)

    def step(n, now, later):
        @pl.when(n >= 2)
        def _():
            give(n - 2)

        product(n + 1, later)
        fold(n, now)
        half_copy(n).start()

    def collect(n, _):
        step(2 * n, sums_a, sums_b)
        step(2 * n + 1, sums_b, sums_a)
        return 0

    last = RAD // 2 - 1
    lax.fori_loop(0, last // 2, collect, 0)
    give(last - 3)
    product(last, sums_b)
    fold(last - 1, sums_a)
    half_copy(last - 1).start()
    fold(last, sums_b)
    half_copy(last).start()
    for n in (last - 2, last - 1, last):
        give(n)

    def take(k, acc):
        c = chip ^ k
        remote(send.at[c], landed.at[c], put_send.at[c], put_recv.at[c], 2 * c + core).wait_recv()
        return acc + landed[c].astype(F32)

    acc = lax.fori_loop(1, CHIPS, take, send[chip].astype(F32))

    quarter = 2 * lax.rem(chip, 2) + core
    row = lax.broadcasted_iota(jnp.int32, (PIECE, ANG), 0)
    lane = lax.broadcasted_iota(jnp.int32, (PIECE, ANG), 1)
    which = jnp.where(row < 24, 24 * quarter + row, 96 + quarter)
    total = acc[25:26] + acc[26:27] + acc[30:31] + acc[31:32]
    total = jnp.sum(jnp.where(lane == which, total, 0.0), axis=1, keepdims=True)
    gathered[chip] = (acc / jnp.maximum(total, 1.0)).astype(BF16)
    evidence[...] = acc[27:28] + acc[28:29] + acc[29:30]

    def share(c, to):
        return remote(gathered.at[c], gathered.at[c], get_send.at[to], get_recv.at[c], 2 * to + core)

    def pass_on(c):
        return remote(gathered.at[c], crossed.at[c], cross_send.at[c], cross_recv.at[c], partner)

    def spread(k, _):
        share(chip, chip ^ k).start()
        return 0

    lax.fori_loop(1, CHIPS, spread, 0)
    pass_on(chip).start()

    def write(piece, c, k):
        r = c // 2
        q = 2 * lax.rem(c, 2) + k
        wide = piece.astype(F32)
        means[pl.ds(24 * RAD * q + r, 24, stride=RAD), :] = wide[:24]
        means[pl.ds((96 + q) * RAD + r, 1), :] = wide[24:25]

    write(gathered[chip], chip, core)

    def pick(k, _):
        c = chip ^ k
        share(c, c).wait_recv()
        pass_on(c).start()
        write(gathered[c], c, core)
        return 0

    lax.fori_loop(1, CHIPS, pick, 0)

    def cross(k, _):
        c = chip ^ k
        pass_on(c).wait_recv()
        write(crossed[c], c, 1 - core)
        return 0

    lax.fori_loop(0, CHIPS, cross, 0)

    def drain_half(n, _):
        half_copy(n).wait_send()
        return 0

    lax.fori_loop(0, RAD // 2, drain_half, 0)
    def drain(k, _):
        c = chip ^ k
        put(c, chip).wait_send()
        share(chip, c).wait_send()
        pass_on(c).wait_send()
        return 0

    lax.fori_loop(1, CHIPS, drain, 0)
    pass_on(chip).wait_send()


def iteration(micrographs, positions, counts, dest_rows, templates):
    mics, slots = dest_rows.shape
    parts = mics * slots
    cells = RAD * ANG
    ys, xs = sample_points()
    vmem = pl.BlockSpec(memory_space=pltpu.VMEM)
    smem = pl.BlockSpec(memory_space=pltpu.SMEM)
    return pl.pallas_call(
        iteration_kernel,
        out_shape=(
            jax.ShapeDtypeStruct((CLASSES * RAD, ANG), F32),
            jax.ShapeDtypeStruct((1, ANG), F32),
        ),
        in_specs=[smem, smem, pl.BlockSpec(memory_space=pl.ANY), vmem, vmem, vmem, vmem],
        out_specs=(vmem, vmem),
        scratch_shapes=[
            pltpu.VMEM((DEVICES * 8, ANG), F32),
            pltpu.VMEM((2, 1024, 1024), BF16),
            pltpu.VMEM((8, 1024, ANG), F32),
            pltpu.VMEM((BOX // 2 * parts, ANG), F32),
            pltpu.VMEM((parts, BOX * BOX), BF16),
            pltpu.VMEM((2, 34 * BOX, 2 * ANG), BF16),
            pltpu.VMEM((CPAD * RAD, ANG), F32),
            pltpu.VMEM((CPAD * RAD, ANG), BF16),
            pltpu.VMEM((ANG, BASE * ANG), BF16),
            pltpu.VMEM((NROWS, cells), BF16),
            pltpu.VMEM((NROWS, ANG), F32),
            pltpu.VMEM((QROT * parts, cells), BF16),
            pltpu.VMEM((NROWS, QROT * parts), F32),
            pltpu.VMEM((NROWS, QROT * parts), BF16),
            pltpu.VMEM((NROWS, ANG), F32),
            pltpu.VMEM((NROWS, 2 * ANG), F32),
            pltpu.VMEM((NROWS, 2 * ANG), F32),
            pltpu.VMEM((2, CHIPS, PIECE, ANG), BF16),
        ]
        + [pltpu.VMEM((CHIPS, PIECE, ANG), BF16)] * 5
        + [pltpu.SemaphoreType.DMA((n,)) for n in (2, 16, 16, 64, 64, 64, 64, 64, 64)],
        compiler_params=pltpu.CompilerParams(
            vmem_limit_bytes=60 * 1024 * 1024, collective_id=0, has_side_effects=True
        ),
        name="iteration",
    )(positions, counts, micrographs, dest_rows, jnp.asarray(ys), jnp.asarray(xs), templates)
def on_device(micrographs, positions, counts, dest_rows, templates):
    means, loglik = iteration(micrographs, positions, counts, dest_rows, templates)
    return means.reshape(CLASSES, RAD, ANG), loglik.reshape(ANG)


def solution(mesh):
    P = jax.sharding.PartitionSpec
    return jax.shard_map(
        on_device,
        mesh=mesh,
        in_specs=(P("dev", None, None), P(None, "dev", None), P("dev"), P("dev", None), P()),
        out_specs=(P(), P("dev")),
        check_vma=False,
    )
```

```python
import functools
import numpy as np
import jax
import jax.numpy as jnp
from jax import lax
from jax.experimental import pallas as pl
from jax.experimental.pallas import tpu as pltpu

BOX = 64
RAD = 32
ANG = 128
CLASSES = 100
ROTS = 36
CPAD = 104
QROT = 4
BASE = 9
NROWS = 4 * 2 * CPAD + 112
DEVICES = 128
CHIPS = DEVICES // 2
PIECE = 32
F32 = jnp.float32
BF16 = jnp.bfloat16


def sample_points():
    center = np.float32((BOX - 1) / 2.0)
    radius = (np.arange(RAD, dtype=np.float32) + np.float32(0.5)) * np.float32(BOX / 2.0 - 1.0) / np.float32(RAD)
    theta = np.float32(2.0 * np.pi) * np.arange(ANG, dtype=np.float32) / np.float32(ANG)
    ys = (center + radius[:, None] * np.sin(theta)[None, :]).reshape(1, -1)
    xs = (center + radius[:, None] * np.cos(theta)[None, :]).reshape(1, -1)
    def ordered(v):
        v = v.astype(np.float32).reshape(RAD // 4, 2, 2, 2, ANG // 2)
        v = v.transpose(0, 3, 1, 2, 4)
        v = np.stack([v[:, 0], v[:, 1, :, ::-1]], axis=1)
        return v.reshape(1, -1)

    return ordered(ys), ordered(xs)


def rotation_taps():
    a = np.arange(ANG, dtype=np.float32)
    taps = []
    for k in range(BASE):
        shift = np.float32(k) * np.float32(ANG) / np.float32(ROTS)
        d = a - np.float32(0) - shift
        d = d - ANG * np.floor(d / np.float32(ANG) + np.float32(0.5))
        w = np.maximum(np.float32(0), np.float32(1) - np.abs(d)).astype(jnp.bfloat16).astype(np.float32)
        first = int(32 * k // 9)
        taps.append((first, float(w[first]), float(w[(first + 1) % ANG]) if k else 0.0))
    return taps


TAPS = rotation_taps()


def turned_rows(x, i):
    if i == 8:
        return x[8 * CPAD : 9 * CPAD]
    pair = x[(i // 2) * 2 * CPAD : (i // 2 + 1) * 2 * CPAD].reshape(CPAD // 8, 16, x.shape[1])
    return pair[:, 8 * (i % 2) : 8 * (i % 2) + 8].reshape(CPAD, x.shape[1])


def remote(src, dst, send_sem, recv_sem, device):
    return pltpu.make_async_remote_copy(
        src_ref=src,
        dst_ref=dst,
        send_sem=send_sem,
        recv_sem=recv_sem,
        device_id=(device,),
        device_id_type=pl.DeviceIdType.MESH,
    )


def iteration_kernel(pos, counts, mic, dest, ys, xs, tmpl, means, evidence, extra, raw, planes, flat, boxes, wtile, tflat, byrad, rmat, rot, esum, shifted, scores, weights, tsum, sums_a, sums_b, out, half, send, landed, gathered, crossed, table, sems,
                     half_send, half_recv, put_send, put_recv, get_send, get_recv, cross_send, cross_recv):
    mics = mic.shape[0]
    slots = pos.shape[2]
    parts = mics * slots

    me = lax.axis_index("dev")
    core = lax.rem(me, 2)
    chip = me // 2
    partner = me + 1 - 2 * core

    barrier = pltpu.get_barrier_semaphore()
    pl.semaphore_signal(barrier, inc=1, device_id=(partner,), device_id_type=pl.DeviceIdType.MESH)

    def greet(k, _):
        pl.semaphore_signal(
            barrier, inc=1, device_id=(2 * (chip ^ k) + core,), device_id_type=pl.DeviceIdType.MESH
        )
        return 0

    lax.fori_loop(1, CHIPS, greet, 0)

    def fetch(i):
        return pltpu.make_async_copy(mic.at[i], raw.at[i % 2], sems.at[i % 2])

    fetch(0).start()
    fetch(1).start()

    lane1 = lax.broadcasted_iota(jnp.int32, (1, ANG), 1)

    away = lax.broadcasted_iota(jnp.int32, (ANG, ANG), 1) - lax.broadcasted_iota(jnp.int32, (ANG, ANG), 0)
    for i, (first, w0, w1) in enumerate(TAPS):
        step = (away - first) & 127
        turn = jnp.where(step == 0, w0, jnp.where(step == 1, w1, 0.0))
        rmat[:, i * ANG : (i + 1) * ANG] = turn.astype(BF16)
    tflat[pl.ds(CLASSES * RAD, (CPAD - CLASSES) * RAD), :] = jnp.zeros(((CPAD - CLASSES) * RAD, ANG), F32)
    tflat[pl.ds(0, CLASSES * RAD), :] = tmpl[...].reshape(CLASSES * RAD, ANG).astype(F32)
    esum[...] = jnp.zeros_like(esum)
    tiles = CPAD // 8

    def regroup(n, _):
        pair = [tflat[pl.ds(2 * n + h, CPAD, stride=RAD), :] for h in range(2)]
        byrad[pl.ds(pl.multiple_of(n * 2 * CPAD, 16), 2 * CPAD), :] = jnp.concatenate(pair, axis=0).astype(BF16)
        return 0

    lax.fori_loop(0, RAD // 2, regroup, 0, unroll=2)

    def rotate_block(n, _):
        few = 4
        block = byrad[pl.ds(pl.multiple_of(n * few * CPAD, 16), few * CPAD), :]
        for k in range(5):
            start, height = (k * 2 * CPAD, 2 * CPAD) if k < 4 else (8 * CPAD, 112)
            wide = jnp.dot(block, rmat[:, k * 2 * ANG : min(k * 2 + 2, 9) * ANG], preferred_element_type=F32)
            total = jnp.zeros((height, ANG), F32)
            for h in range(few):
                some = wide[h * CPAD : (h + 1) * CPAD]
                if k < 4:
                    some = [some[:, m * ANG : (m + 1) * ANG].reshape(tiles, 8, ANG) for m in range(2)]
                    some = jnp.concatenate(some, axis=1).reshape(2 * CPAD, ANG)
                else:
                    some = jnp.concatenate([some, jnp.zeros((8, ANG), F32)], axis=0)
                some = some.astype(BF16)
                col = pl.ds(pl.multiple_of((n * few + h) * ANG, ANG), ANG)
                rot[start : start + height, col] = some
                some = some.astype(F32)
                total += some * some
            esum[start : start + height, :] += total
        return 0

    lax.fori_loop(0, RAD // 4, rotate_block, 0)

    lanes = lax.broadcasted_iota(jnp.int32, (BOX // 2, ANG), 1)
    for i in range(mics):
        fetch(i).wait()
        for t in range(8):
            planes[t, :, :] = raw[i % 2, :, t * ANG : (t + 1) * ANG].astype(F32)
        if i + 2 < mics:
            fetch(i + 2).start()

        def cut(j, _, i=i):
            y = pos[0, i, j]
            x = pos[1, i, j]
            t = x >> 7
            s = x & 127
            t1 = jnp.minimum(t + 1, 7)
            even = pl.ds(y, BOX // 2, stride=2)
            odd = pl.ds(y + 1, BOX // 2, stride=2)
            keep = lanes >= s
            e = jnp.where(keep, planes[t, even, :], planes[t1, even, :])
            o = jnp.where(keep, planes[t, odd, :], planes[t1, odd, :])
            e = pltpu.roll(e, (ANG - s) & 127, 1)
            o = pltpu.roll(o, (ANG + BOX - s) & 127, 1)
            flat[pl.ds(pl.multiple_of((i * slots + j) * (BOX // 2), BOX // 2), BOX // 2), :] = jnp.where(lanes < BOX, e, o)
            return 0

        lax.fori_loop(0, slots, cut, 0, unroll=8)

    for s in range(BOX // 2):
        boxes[:, s * ANG : (s + 1) * ANG] = flat[pl.ds(s, parts, stride=BOX // 2), :].astype(BF16)

    pix = lax.broadcasted_iota(jnp.int32, (BOX, 2 * ANG), 0).astype(F32)
    left = lax.broadcasted_iota(jnp.int32, (parts, ANG), 1) < BOX
    for g in range(RAD // 4):
        radius = (4 * g + 3.5) * (BOX / 2.0 - 1.0) / RAD
        reach = (int(np.floor(31.501 + radius)) + 3) // 2 * 2
        halves = []
        for side in range(2):
            low, high = (30, reach) if side == 0 else (BOX - reach, 34)
            cols = slice((2 * g + side) * 2 * ANG, (2 * g + side + 1) * 2 * ANG)
            rw = jnp.maximum(0.0, 1.0 - jnp.abs(pix - ys[:, cols]))
            cw = jnp.maximum(0.0, 1.0 - jnp.abs(pix - xs[:, cols]))
            w = wtile.at[side]
            for u in range(low, high):
                w[(u - low) * BOX : (u - low + 1) * BOX, :] = (rw[u : u + 1, :] * cw).astype(BF16)
            halves.append(
                jnp.dot(
                    boxes[:, low * BOX : high * BOX],
                    w[: (high - low) * BOX, :],
                    preferred_element_type=F32,
                )
            )
        for m in range(2):
            upper = halves[0][:, m * ANG : (m + 1) * ANG]
            lower = halves[1][:, m * ANG : (m + 1) * ANG]
            for h in range(2):
                whole = jnp.where(left, upper, lower) if h == 0 else jnp.where(left, lower, upper)
                c0 = (4 * g + 2 * m + h) * ANG
                for j in range(QROT):
                    turn = (BOX * h - 32 * j) % ANG
                    part = pltpu.roll(whole, turn, 1) if turn else whole
                    shifted[j * parts : (j + 1) * parts, c0 : c0 + ANG] = part.astype(BF16)

    rows = lax.broadcasted_iota(jnp.int32, (NROWS, 1), 0)
    energy = 0.5 * jnp.sum(esum[...], axis=1, keepdims=True)
    paired = lax.rem(rows >> 4, 13) * 8 + (rows & 7)
    pad = jnp.where(rows < 8 * CPAD, paired, rows - 8 * CPAD) >= CLASSES
    energy = jnp.where(pad, 1e30, energy)

    def score(j, peak):
        rows_j = pl.ds(pl.multiple_of(j * parts, parts), parts)
        prod = lax.dot_general(rot[...], shifted[rows_j, :], (((1,), (1,)), ((), ())), preferred_element_type=F32)
        prod = prod - energy
        scores[:, rows_j] = prod
        return jnp.maximum(peak, jnp.max(prod, axis=0, keepdims=True))

    peak = lax.fori_loop(0, QROT, score, jnp.full((1, parts), -3e38, F32))
    peak4 = jnp.concatenate([peak] * QROT, axis=1)

    def expo(n, acc):
        rr = pl.ds(pl.multiple_of(n * 16, 16), 16)
        e = jnp.exp(scores[rr, :] - peak4)
        scores[rr, :] = e
        return acc + e[:8] + e[8:]

    acc = lax.fori_loop(0, NROWS // 16, expo, jnp.zeros((8, QROT * parts), F32))
    norm = jnp.sum(acc, axis=0, keepdims=True)
    norm = sum(norm[:, j * parts : (j + 1) * parts] for j in range(QROT))
    loglik = peak + jnp.log(norm)

    lane = lax.broadcasted_iota(jnp.int32, (1, parts), 1)
    target = jnp.concatenate([dest[i : i + 1, :] for i in range(mics)], axis=1)
    live = target >= 0
    for i in range(mics):
        live = live & ((lane < i * slots + counts[i]) | (lane >= (i + 1) * slots))
    inv = jnp.where(live, 1.0 / norm, 0.0)
    inv4 = jnp.concatenate([inv] * QROT, axis=1)

    def weigh(n, _):
        rr = pl.ds(pl.multiple_of(n * 16, 16), 16)
        w = (scores[rr, :] * inv4).astype(BF16)
        weights[rr, :] = w
        wide = w.astype(F32)
        tsum[rr, :] = sum(wide[:, k * ANG : (k + 1) * ANG] for k in range(QROT * parts // ANG))
        return 0

    lax.fori_loop(0, NROWS // 16, weigh, 0)
    tot = jnp.sum(sum(turned_rows(tsum[...], i) for i in range(BASE)), axis=1, keepdims=True)
    spot = lax.broadcasted_iota(jnp.int32, (CPAD, ANG), 0) == lax.broadcasted_iota(jnp.int32, (CPAD, ANG), 1)
    tot = jnp.sum(jnp.where(spot, tot, 0.0), axis=0, keepdims=True)
    high = tot.astype(BF16).astype(F32)
    first = core == 0
    extra[...] = jnp.zeros_like(extra)
    for value, here, there in ((high, 1, 6), (tot - high, 2, 7)):
        value = jnp.broadcast_to(value, (DEVICES, ANG))
        extra[pl.ds(here, DEVICES, stride=8), :] = jnp.where(first, value, 0.0)
        extra[pl.ds(there, DEVICES, stride=8), :] = jnp.where(first, 0.0, value)

    which = lax.broadcasted_iota(jnp.int32, (ANG, parts), 0)
    owner = jnp.where((which == (target >> 7)) & live, 1.0, 0.0)
    row = jnp.where(which == (target & 127), 1.0, 0.0).astype(BF16)
    rest = loglik
    for k in range(3):
        piece = rest.astype(BF16).astype(F32)
        placed = lax.dot_general((owner * piece).astype(BF16), row, (((1,), (1,)), ((), ())), preferred_element_type=F32)
        extra[pl.ds(3 + k, DEVICES, stride=8), :] = placed
        rest = rest - piece

    top = lax.broadcasted_iota(jnp.int32, (8, ANG), 0)

    def turn(n):
        return n ^ (chip // 4)

    def product(n, into):
        g = turn(n)
        cols = pl.ds(pl.multiple_of(g * 2 * ANG, 2 * ANG), 2 * ANG)
        into[...] = jnp.dot(weights[...], shifted[:, cols], preferred_element_type=F32)

    def fold(n, source):
        g = turn(n)
        for k in range(2):
            sum0 = jnp.zeros((CPAD, ANG), F32)
            sum1 = jnp.zeros((CPAD, ANG), F32)
            half = source[:, k * ANG : (k + 1) * ANG]
            for i, (first, w0, w1) in enumerate(TAPS):
                q = turned_rows(half, i)
                if first:
                    q = pltpu.roll(q, ANG - first, 1)
                sum0 += w0 * q
                if w1:
                    sum1 += w1 * q
            total = sum0 + pltpu.roll(sum1, ANG - 1, 1)
            r = 2 * g + k
            for q in range(4):
                tail = total[96:] if q == 0 else pltpu.roll(total[96:], 8 - q, 0)
                spare = extra[pl.ds(pl.multiple_of((4 * r + q) * 8, 8), 8), :]
                tail = jnp.where(top == 0, tail, spare)
                piece = jnp.concatenate([total[24 * q : 24 * q + 24], tail], axis=0)
                out[q % 2, 2 * r + q // 2, :, :] = piece.astype(BF16)

    def half_copy(n):
        at = pl.ds(4 * turn(n), 4)
        return remote(out.at[1 - core, at], half.at[at], half_send, half_recv.at[n], partner)

    def put(c):
        return remote(send.at[c], landed.at[chip], put_send, put_recv, 2 * c + core)

    def give(n, home=False):
        half_copy(n).wait_recv()
        for m in range(4):
            c = 4 * turn(n) + m
            send[c] = (out[core, c].astype(F32) + half[c].astype(F32)).astype(BF16)
        if home:
            landed[chip] = send[chip]
        for m in range(4):
            c = 4 * turn(n) + m
            if home:

                @pl.when(c != chip)
                def _():
                    put(c).start()

            else:
                put(c).start()

    def pair(n):
        product(2 * n + 1, sums_b)
        fold(2 * n, sums_a)
        product(2 * n + 2, sums_a)
        fold(2 * n + 1, sums_b)
        half_copy(2 * n).start()
        half_copy(2 * n + 1).start()

    def alone(n, _):
        pair(n)
        return 0

    def sending(n, _):
        pair(n)
        give(2 * n - 2)
        give(2 * n - 1)
        return 0

    last = RAD // 2 - 1
    product(0, sums_a)
    pl.semaphore_wait(barrier, CHIPS)
    lax.fori_loop(0, 2, alone, 0)
    give(0, home=True)
    give(1)
    lax.fori_loop(2, last // 2, sending, 0)
    product(last, sums_b)
    fold(last - 1, sums_a)
    half_copy(last - 1).start()
    give(last - 3)
    give(last - 2)
    fold(last, sums_b)
    half_copy(last).start()
    give(last - 1)
    give(last)

    others = pl.ds(0, CHIPS - 1)
    remote(send.at[others], landed.at[others], put_send, put_recv, partner).wait_recv()

    def take(k, acc):
        return acc + sum(landed[8 * k + m].astype(F32) for m in range(8))

    acc = lax.fori_loop(0, CHIPS // 8, take, jnp.zeros((PIECE, ANG), F32))

    quarter = 2 * lax.rem(chip, 2) + core
    row = lax.broadcasted_iota(jnp.int32, (PIECE, ANG), 0)
    lane = lax.broadcasted_iota(jnp.int32, (PIECE, ANG), 1)
    which = jnp.where(row < 24, 24 * quarter + row, 96 + quarter)
    total = acc[25:26] + acc[26:27] + acc[30:31] + acc[31:32]
    total = jnp.sum(jnp.where(lane == which, total, 0.0), axis=1, keepdims=True)
    gathered[chip] = (acc / jnp.maximum(total, 1.0)).astype(BF16)
    evidence[...] = acc[27:28] + acc[28:29] + acc[29:30]

    def share(slot, to):
        return remote(gathered.at[slot], gathered.at[slot], get_send, get_recv.at[slot], 2 * to + core)

    def pass_on(c):
        return remote(gathered.at[c], crossed.at[c], cross_send, cross_recv.at[c], partner)

    def spread(k, _):
        share(chip, chip ^ k).start()
        return 0

    lax.fori_loop(1, CHIPS, spread, 0, unroll=3)
    pass_on(chip).start()

    def write(piece, c, k):
        r = c // 2
        q = 2 * lax.rem(c, 2) + k
        wide = piece.astype(F32)
        table[pl.ds(24 * RAD * q + r, 24, stride=RAD), :] = wide[:24]
        table[pl.ds((96 + q) * RAD + r, 1), :] = wide[24:25]

    def cross(k):
        c = chip ^ k
        pass_on(c).wait_recv()
        write(crossed[c], c, 1 - core)

    def pick(k):
        c = chip ^ k
        share(c, c).wait_recv()
        pass_on(c).start()
        write(gathered[c], c, core)

    lag = 6
    write(gathered[chip], chip, core)

    def early(k, _):
        pick(k)
        return 0

    def both(k, _):
        pick(k)
        cross(k - lag)
        return 0

    def late(k, _):
        cross(k)
        return 0

    lax.fori_loop(1, lag, early, 0)
    lax.fori_loop(lag, CHIPS, both, 0)
    lax.fori_loop(CHIPS - lag, CHIPS, late, 0)
    means[...] = table[...].astype(BF16)

    remote(out.at[1 - core], half, half_send, half_recv.at[0], partner).wait_send()
    remote(send.at[others], landed.at[others], put_send, put_recv, partner).wait_send()
    remote(gathered.at[others], landed.at[others], get_send, put_recv, partner).wait_send()
    remote(gathered, crossed, cross_send, put_recv, partner).wait_send()


def iteration(micrographs, positions, counts, dest_rows, templates):
    mics, slots = dest_rows.shape
    parts = mics * slots
    cells = RAD * ANG
    ys, xs = sample_points()
    vmem = pl.BlockSpec(memory_space=pltpu.VMEM)
    smem = pl.BlockSpec(memory_space=pltpu.SMEM)
    one = pltpu.SemaphoreType.DMA
    many = pltpu.SemaphoreType.DMA((CHIPS,))
    return pl.pallas_call(
        iteration_kernel,
        out_shape=(
            jax.ShapeDtypeStruct((CLASSES * RAD, ANG), BF16),
            jax.ShapeDtypeStruct((1, ANG), F32),
        ),
        in_specs=[smem, smem, pl.BlockSpec(memory_space=pl.ANY), vmem, vmem, vmem, vmem],
        out_specs=(vmem, vmem),
        scratch_shapes=[
            pltpu.VMEM((DEVICES * 8, ANG), F32),
            pltpu.VMEM((2, 1024, 1024), BF16),
            pltpu.VMEM((8, 1024, ANG), F32),
            pltpu.VMEM((BOX // 2 * parts, ANG), F32),
            pltpu.VMEM((parts, BOX * BOX), BF16),
            pltpu.VMEM((2, 34 * BOX, 2 * ANG), BF16),
            pltpu.VMEM((CPAD * RAD, ANG), F32),
            pltpu.VMEM((CPAD * RAD, ANG), BF16),
            pltpu.VMEM((ANG, BASE * ANG), BF16),
            pltpu.VMEM((NROWS, cells), BF16),
            pltpu.VMEM((NROWS, ANG), F32),
            pltpu.VMEM((QROT * parts, cells), BF16),
            pltpu.VMEM((NROWS, QROT * parts), F32),
            pltpu.VMEM((NROWS, QROT * parts), BF16),
            pltpu.VMEM((NROWS, ANG), F32),
            pltpu.VMEM((NROWS, 2 * ANG), F32),
            pltpu.VMEM((NROWS, 2 * ANG), F32),
            pltpu.VMEM((2, CHIPS, PIECE, ANG), BF16),
        ]
        + [pltpu.VMEM((CHIPS, PIECE, ANG), BF16)] * 5
        + [pltpu.VMEM((CLASSES * RAD, ANG), F32), pltpu.SemaphoreType.DMA((2,))]
        + [one, pltpu.SemaphoreType.DMA((RAD // 2,)), one, one, one, many, one, many],
        compiler_params=pltpu.CompilerParams(
            vmem_limit_bytes=60 * 1024 * 1024, collective_id=0, has_side_effects=True
        ),
        name="iteration",
    )(positions, counts, micrographs, dest_rows, jnp.asarray(ys), jnp.asarray(xs), templates)
def on_device(micrographs, positions, counts, dest_rows, templates):
    means, loglik = iteration(micrographs, positions, counts, dest_rows, templates)
    return means.reshape(CLASSES, RAD, ANG).astype(F32), loglik.reshape(ANG)


def solution(mesh):
    P = jax.sharding.PartitionSpec
    return jax.shard_map(
        on_device,
        mesh=mesh,
        in_specs=(P("dev", None, None), P(None, "dev", None), P("dev"), P("dev", None), P()),
        out_specs=(P(), P("dev")),
        check_vma=False,
    )
```

```python
import functools
import numpy as np
import jax
import jax.numpy as jnp
from jax import lax
from jax.experimental import pallas as pl
from jax.experimental.pallas import tpu as pltpu

BOX = 64
RAD = 32
ANG = 128
CLASSES = 100
ROTS = 36
CPAD = 104
QROT = 4
BASE = 9
NROWS = 4 * 2 * CPAD + 112
DEVICES = 128
CHIPS = DEVICES // 2
PIECE = 32
F32 = jnp.float32
BF16 = jnp.bfloat16


def sample_points():
    center = np.float32((BOX - 1) / 2.0)
    radius = (np.arange(RAD, dtype=np.float32) + np.float32(0.5)) * np.float32(BOX / 2.0 - 1.0) / np.float32(RAD)
    theta = np.float32(2.0 * np.pi) * np.arange(ANG, dtype=np.float32) / np.float32(ANG)
    ys = (center + radius[:, None] * np.sin(theta)[None, :]).reshape(1, -1)
    xs = (center + radius[:, None] * np.cos(theta)[None, :]).reshape(1, -1)
    def ordered(v):
        v = v.astype(np.float32).reshape(RAD // 4, 2, 2, 2, ANG // 2)
        v = v.transpose(0, 3, 1, 2, 4)
        v = np.stack([v[:, 0], v[:, 1, :, ::-1]], axis=1)
        return v.reshape(1, -1)

    return ordered(ys), ordered(xs)


def rotation_taps():
    a = np.arange(ANG, dtype=np.float32)
    taps = []
    for k in range(BASE):
        shift = np.float32(k) * np.float32(ANG) / np.float32(ROTS)
        d = a - np.float32(0) - shift
        d = d - ANG * np.floor(d / np.float32(ANG) + np.float32(0.5))
        w = np.maximum(np.float32(0), np.float32(1) - np.abs(d)).astype(jnp.bfloat16).astype(np.float32)
        first = int(32 * k // 9)
        taps.append((first, float(w[first]), float(w[(first + 1) % ANG]) if k else 0.0))
    return taps


TAPS = rotation_taps()


def turned_rows(x, i):
    if i == 8:
        return x[8 * CPAD : 9 * CPAD]
    pair = x[(i // 2) * 2 * CPAD : (i // 2 + 1) * 2 * CPAD].reshape(CPAD // 8, 16, x.shape[1])
    return pair[:, 8 * (i % 2) : 8 * (i % 2) + 8].reshape(CPAD, x.shape[1])


def remote(src, dst, send_sem, recv_sem, device):
    return pltpu.make_async_remote_copy(
        src_ref=src,
        dst_ref=dst,
        send_sem=send_sem,
        recv_sem=recv_sem,
        device_id=(device,),
        device_id_type=pl.DeviceIdType.MESH,
    )


def iteration_kernel(pos, counts, mic, dest, ys, xs, tmpl, means, evidence, extra, raw, planes, flat, boxes, wtile, tflat, byrad, rmat, rot, esum, shifted, scores, weights, tsum, sums_a, sums_b, out, half, send, landed, gathered, crossed, table, sems,
                     half_send, half_recv, put_send, put_recv, get_send, get_recv, cross_send, cross_recv):
    mics = mic.shape[0]
    slots = pos.shape[2]
    parts = mics * slots

    me = lax.axis_index("dev")
    core = lax.rem(me, 2)
    chip = me // 2
    partner = me + 1 - 2 * core

    barrier = pltpu.get_barrier_semaphore()
    pl.semaphore_signal(barrier, inc=1, device_id=(partner,), device_id_type=pl.DeviceIdType.MESH)

    def greet(k, _):
        pl.semaphore_signal(
            barrier, inc=1, device_id=(2 * (chip ^ k) + core,), device_id_type=pl.DeviceIdType.MESH
        )
        return 0

    lax.fori_loop(1, CHIPS, greet, 0)

    def fetch(i):
        return pltpu.make_async_copy(mic.at[i], raw.at[i % 2], sems.at[i % 2])

    fetch(0).start()
    fetch(1).start()

    lane1 = lax.broadcasted_iota(jnp.int32, (1, ANG), 1)

    away = lax.broadcasted_iota(jnp.int32, (ANG, ANG), 1) - lax.broadcasted_iota(jnp.int32, (ANG, ANG), 0)
    for i, (first, w0, w1) in enumerate(TAPS):
        step = (away - first) & 127
        turn = jnp.where(step == 0, w0, jnp.where(step == 1, w1, 0.0))
        rmat[:, i * ANG : (i + 1) * ANG] = turn.astype(BF16)
    tflat[pl.ds(CLASSES * RAD, (CPAD - CLASSES) * RAD), :] = jnp.zeros(((CPAD - CLASSES) * RAD, ANG), F32)
    tflat[pl.ds(0, CLASSES * RAD), :] = tmpl[...].reshape(CLASSES * RAD, ANG).astype(F32)
    esum[...] = jnp.zeros_like(esum)
    tiles = CPAD // 8

    def regroup(n, _):
        pair = [tflat[pl.ds(2 * n + h, CPAD, stride=RAD), :] for h in range(2)]
        byrad[pl.ds(pl.multiple_of(n * 2 * CPAD, 16), 2 * CPAD), :] = jnp.concatenate(pair, axis=0).astype(BF16)
        return 0

    lax.fori_loop(0, RAD // 2, regroup, 0, unroll=2)

    def rotate_block(n, _):
        few = 4
        block = byrad[pl.ds(pl.multiple_of(n * few * CPAD, 16), few * CPAD), :]
        for k in range(5):
            start, height = (k * 2 * CPAD, 2 * CPAD) if k < 4 else (8 * CPAD, 112)
            wide = jnp.dot(block, rmat[:, k * 2 * ANG : min(k * 2 + 2, 9) * ANG], preferred_element_type=F32)
            total = jnp.zeros((height, ANG), F32)
            for h in range(few):
                some = wide[h * CPAD : (h + 1) * CPAD]
                if k < 4:
                    some = [some[:, m * ANG : (m + 1) * ANG].reshape(tiles, 8, ANG) for m in range(2)]
                    some = jnp.concatenate(some, axis=1).reshape(2 * CPAD, ANG)
                else:
                    some = jnp.concatenate([some, jnp.zeros((8, ANG), F32)], axis=0)
                some = some.astype(BF16)
                col = pl.ds(pl.multiple_of((n * few + h) * ANG, ANG), ANG)
                rot[start : start + height, col] = some
                some = some.astype(F32)
                total += some * some
            esum[start : start + height, :] += total
        return 0

    lax.fori_loop(0, RAD // 4, rotate_block, 0)

    lanes = lax.broadcasted_iota(jnp.int32, (BOX // 2, ANG), 1)
    for i in range(mics):
        fetch(i).wait()
        for t in range(8):
            planes[t, :, :] = raw[i % 2, :, t * ANG : (t + 1) * ANG].astype(F32)
        if i + 2 < mics:
            fetch(i + 2).start()

        def cut(j, _, i=i):
            y = pos[0, i, j]
            x = pos[1, i, j]
            t = x >> 7
            s = x & 127
            t1 = jnp.minimum(t + 1, 7)
            even = pl.ds(y, BOX // 2, stride=2)
            odd = pl.ds(y + 1, BOX // 2, stride=2)
            keep = lanes >= s
            e = jnp.where(keep, planes[t, even, :], planes[t1, even, :])
            o = jnp.where(keep, planes[t, odd, :], planes[t1, odd, :])
            e = pltpu.roll(e, (ANG - s) & 127, 1)
            o = pltpu.roll(o, (ANG + BOX - s) & 127, 1)
            flat[pl.ds(pl.multiple_of((i * slots + j) * (BOX // 2), BOX // 2), BOX // 2), :] = jnp.where(lanes < BOX, e, o)
            return 0

        lax.fori_loop(0, slots, cut, 0, unroll=8)

    for s in range(BOX // 2):
        boxes[:, s * ANG : (s + 1) * ANG] = flat[pl.ds(s, parts, stride=BOX // 2), :].astype(BF16)

    pix = lax.broadcasted_iota(jnp.int32, (BOX, 2 * ANG), 0).astype(F32)
    left = lax.broadcasted_iota(jnp.int32, (parts, ANG), 1) < BOX
    for g in range(RAD // 4):
        radius = (4 * g + 3.5) * (BOX / 2.0 - 1.0) / RAD
        reach = (int(np.floor(31.501 + radius)) + 3) // 2 * 2
        halves = []
        for side in range(2):
            low, high = (30, reach) if side == 0 else (BOX - reach, 34)
            cols = slice((2 * g + side) * 2 * ANG, (2 * g + side + 1) * 2 * ANG)
            rw = jnp.maximum(0.0, 1.0 - jnp.abs(pix - ys[:, cols]))
            cw = jnp.maximum(0.0, 1.0 - jnp.abs(pix - xs[:, cols]))
            w = wtile.at[side]
            for u in range(low, high):
                w[(u - low) * BOX : (u - low + 1) * BOX, :] = (rw[u : u + 1, :] * cw).astype(BF16)
            halves.append(
                jnp.dot(
                    boxes[:, low * BOX : high * BOX],
                    w[: (high - low) * BOX, :],
                    preferred_element_type=F32,
                )
            )
        for m in range(2):
            upper = halves[0][:, m * ANG : (m + 1) * ANG]
            lower = halves[1][:, m * ANG : (m + 1) * ANG]
            for h in range(2):
                whole = jnp.where(left, upper, lower) if h == 0 else jnp.where(left, lower, upper)
                c0 = (4 * g + 2 * m + h) * ANG
                for j in range(QROT):
                    turn = (BOX * h - 32 * j) % ANG
                    part = pltpu.roll(whole, turn, 1) if turn else whole
                    shifted[j * parts : (j + 1) * parts, c0 : c0 + ANG] = part.astype(BF16)

    rows = lax.broadcasted_iota(jnp.int32, (NROWS, 1), 0)
    energy = 0.5 * jnp.sum(esum[...], axis=1, keepdims=True)
    paired = lax.rem(rows >> 4, 13) * 8 + (rows & 7)
    pad = jnp.where(rows < 8 * CPAD, paired, rows - 8 * CPAD) >= CLASSES
    energy = jnp.where(pad, 1e30, energy)

    def score(j, peak):
        rows_j = pl.ds(pl.multiple_of(j * parts, parts), parts)
        prod = lax.dot_general(rot[...], shifted[rows_j, :], (((1,), (1,)), ((), ())), preferred_element_type=F32)
        prod = prod - energy
        scores[:, rows_j] = prod
        return jnp.maximum(peak, jnp.max(prod, axis=0, keepdims=True))

    peak = lax.fori_loop(0, QROT, score, jnp.full((1, parts), -3e38, F32))
    peak4 = jnp.concatenate([peak] * QROT, axis=1)

    def expo(n, acc):
        rr = pl.ds(pl.multiple_of(n * 16, 16), 16)
        e = jnp.exp(scores[rr, :] - peak4)
        scores[rr, :] = e
        return acc + e[:8] + e[8:]

    def expo_pair(n, acc):
        return expo(2 * n + 1, expo(2 * n, acc))

    acc = lax.fori_loop(0, NROWS // 32, expo_pair, jnp.zeros((8, QROT * parts), F32))
    acc = expo(NROWS // 16 - 1, acc)
    norm = jnp.sum(acc, axis=0, keepdims=True)
    norm = sum(norm[:, j * parts : (j + 1) * parts] for j in range(QROT))
    loglik = peak + jnp.log(norm)

    lane = lax.broadcasted_iota(jnp.int32, (1, parts), 1)
    target = jnp.concatenate([dest[i : i + 1, :] for i in range(mics)], axis=1)
    live = target >= 0
    for i in range(mics):
        live = live & ((lane < i * slots + counts[i]) | (lane >= (i + 1) * slots))
    inv = jnp.where(live, 1.0 / norm, 0.0)
    inv4 = jnp.concatenate([inv] * QROT, axis=1)

    def weigh(n, _):
        rr = pl.ds(pl.multiple_of(n * 16, 16), 16)
        w = (scores[rr, :] * inv4).astype(BF16)
        weights[rr, :] = w
        wide = w.astype(F32)
        tsum[rr, :] = sum(wide[:, k * ANG : (k + 1) * ANG] for k in range(QROT * parts // ANG))
        return 0

    def weigh_pair(n, _):
        weigh(2 * n, 0)
        return weigh(2 * n + 1, 0)

    lax.fori_loop(0, NROWS // 32, weigh_pair, 0)
    weigh(NROWS // 16 - 1, 0)
    tot = jnp.sum(sum(turned_rows(tsum[...], i) for i in range(BASE)), axis=1, keepdims=True)
    spot = lax.broadcasted_iota(jnp.int32, (CPAD, ANG), 0) == lax.broadcasted_iota(jnp.int32, (CPAD, ANG), 1)
    tot = jnp.sum(jnp.where(spot, tot, 0.0), axis=0, keepdims=True)
    high = tot.astype(BF16).astype(F32)
    first = core == 0
    extra[...] = jnp.zeros_like(extra)
    for value, here, there in ((high, 1, 6), (tot - high, 2, 7)):
        value = jnp.broadcast_to(value, (DEVICES, ANG))
        extra[pl.ds(here, DEVICES, stride=8), :] = jnp.where(first, value, 0.0)
        extra[pl.ds(there, DEVICES, stride=8), :] = jnp.where(first, 0.0, value)

    which = lax.broadcasted_iota(jnp.int32, (ANG, parts), 0)
    owner = jnp.where((which == (target >> 7)) & live, 1.0, 0.0)
    row = jnp.where(which == (target & 127), 1.0, 0.0).astype(BF16)
    rest = loglik
    for k in range(3):
        piece = rest.astype(BF16).astype(F32)
        placed = lax.dot_general((owner * piece).astype(BF16), row, (((1,), (1,)), ((), ())), preferred_element_type=F32)
        extra[pl.ds(3 + k, DEVICES, stride=8), :] = placed
        rest = rest - piece

    top = lax.broadcasted_iota(jnp.int32, (8, ANG), 0)

    def turn(n):
        return (RAD // 2 - 1 - n) ^ (chip // 4)

    def product(n, into):
        g = turn(n)
        cols = pl.ds(pl.multiple_of(g * 2 * ANG, 2 * ANG), 2 * ANG)
        into[...] = jnp.dot(weights[...], shifted[:, cols], preferred_element_type=F32)

    def fold(n, source):
        g = turn(n)
        for k in range(2):
            sum0 = jnp.zeros((CPAD, ANG), F32)
            sum1 = jnp.zeros((CPAD, ANG), F32)
            half = source[:, k * ANG : (k + 1) * ANG]
            for i, (first, w0, w1) in enumerate(TAPS):
                q = turned_rows(half, i)
                if first:
                    q = pltpu.roll(q, ANG - first, 1)
                sum0 += w0 * q
                if w1:
                    sum1 += w1 * q
            total = sum0 + pltpu.roll(sum1, ANG - 1, 1)
            r = 2 * g + k
            for q in range(4):
                tail = total[96:] if q == 0 else pltpu.roll(total[96:], 8 - q, 0)
                spare = extra[pl.ds(pl.multiple_of((4 * r + q) * 8, 8), 8), :]
                tail = jnp.where(top == 0, tail, spare)
                piece = jnp.concatenate([total[24 * q : 24 * q + 24], tail], axis=0)
                out[q % 2, 2 * r + q // 2, :, :] = piece.astype(BF16)

    def half_copy(n):
        at = pl.ds(4 * turn(n), 4)
        return remote(out.at[1 - core, at], half.at[at], half_send, half_recv.at[n], partner)

    def put(c):
        return remote(send.at[c], landed.at[chip], put_send, put_recv, 2 * c + core)

    def give(n, home=False):
        half_copy(n).wait_recv()
        for m in range(4):
            c = 4 * turn(n) + m
            send[c] = (out[core, c].astype(F32) + half[c].astype(F32)).astype(BF16)
        if home:
            landed[chip] = send[chip]
        for m in range(4):
            c = 4 * turn(n) + m
            if home:

                @pl.when(c != chip)
                def _():
                    put(c).start()

            else:
                put(c).start()

    def pair(n):
        product(2 * n + 1, sums_b)
        fold(2 * n, sums_a)
        product(2 * n + 2, sums_a)
        fold(2 * n + 1, sums_b)
        half_copy(2 * n).start()
        half_copy(2 * n + 1).start()

    def alone(n, _):
        pair(n)
        return 0

    def sending(n, _):
        pair(n)
        give(2 * n - 2)
        give(2 * n - 1)
        return 0

    last = RAD // 2 - 1
    product(0, sums_a)
    pl.semaphore_wait(barrier, CHIPS)
    lax.fori_loop(0, 2, alone, 0)
    give(0)
    give(1)
    lax.fori_loop(2, last // 2, sending, 0)
    product(last, sums_b)
    fold(last - 1, sums_a)
    half_copy(last - 1).start()
    give(last - 3)
    give(last - 2)
    fold(last, sums_b)
    half_copy(last).start()
    give(last - 1)
    give(last, home=True)

    others = pl.ds(0, CHIPS - 1)
    remote(send.at[others], landed.at[others], put_send, put_recv, partner).wait_recv()

    def take(k, acc):
        return acc + sum(landed[8 * k + m].astype(F32) for m in range(8))

    acc = lax.fori_loop(0, CHIPS // 8, take, jnp.zeros((PIECE, ANG), F32))

    quarter = 2 * lax.rem(chip, 2) + core
    row = lax.broadcasted_iota(jnp.int32, (PIECE, ANG), 0)
    lane = lax.broadcasted_iota(jnp.int32, (PIECE, ANG), 1)
    which = jnp.where(row < 24, 24 * quarter + row, 96 + quarter)
    total = acc[25:26] + acc[26:27] + acc[30:31] + acc[31:32]
    total = jnp.sum(jnp.where(lane == which, total, 0.0), axis=1, keepdims=True)
    gathered[chip] = (acc / jnp.maximum(total, 1.0)).astype(BF16)
    evidence[...] = acc[27:28] + acc[28:29] + acc[29:30]

    def share(slot, to):
        return remote(gathered.at[slot], gathered.at[slot], get_send, get_recv.at[slot], 2 * to + core)

    def pass_on(c):
        return remote(gathered.at[c], crossed.at[c], cross_send, cross_recv.at[c], partner)

    def spread(k, _):
        share(chip, chip ^ k ^ 42).start()
        return 0

    lax.fori_loop(0, 42, spread, 0, unroll=3)
    lax.fori_loop(43, CHIPS, spread, 0, unroll=3)
    pass_on(chip).start()

    def write(piece, c, k):
        r = c // 2
        q = 2 * lax.rem(c, 2) + k
        wide = piece.astype(F32)
        table[pl.ds(24 * RAD * q + r, 24, stride=RAD), :] = wide[:24]
        table[pl.ds((96 + q) * RAD + r, 1), :] = wide[24:25]

    def cross(k):
        c = chip ^ k
        pass_on(c).wait_recv()
        write(crossed[c], c, 1 - core)

    def pick(k):
        c = chip ^ k
        share(c, c).wait_recv()
        pass_on(c).start()
        write(gathered[c], c, core)

    lag = 6
    write(gathered[chip], chip, core)

    def early(k, _):
        pick(k)
        return 0

    def both(k, _):
        pick(k)
        cross(k - lag)
        return 0

    def late(k, _):
        cross(k)
        return 0

    lax.fori_loop(1, lag, early, 0)
    lax.fori_loop(lag, CHIPS, both, 0)
    lax.fori_loop(CHIPS - lag, CHIPS, late, 0)
    means[...] = table[...].astype(BF16)

    remote(out.at[1 - core], half, half_send, half_recv.at[0], partner).wait_send()
    remote(send.at[others], landed.at[others], put_send, put_recv, partner).wait_send()
    remote(gathered.at[others], landed.at[others], get_send, put_recv, partner).wait_send()
    remote(gathered, crossed, cross_send, put_recv, partner).wait_send()


def iteration(micrographs, positions, counts, dest_rows, templates):
    mics, slots = dest_rows.shape
    parts = mics * slots
    cells = RAD * ANG
    ys, xs = sample_points()
    vmem = pl.BlockSpec(memory_space=pltpu.VMEM)
    smem = pl.BlockSpec(memory_space=pltpu.SMEM)
    one = pltpu.SemaphoreType.DMA
    many = pltpu.SemaphoreType.DMA((CHIPS,))
    return pl.pallas_call(
        iteration_kernel,
        out_shape=(
            jax.ShapeDtypeStruct((CLASSES * RAD, ANG), BF16),
            jax.ShapeDtypeStruct((1, ANG), F32),
        ),
        in_specs=[smem, smem, pl.BlockSpec(memory_space=pl.ANY), vmem, vmem, vmem, vmem],
        out_specs=(vmem, vmem),
        scratch_shapes=[
            pltpu.VMEM((DEVICES * 8, ANG), F32),
            pltpu.VMEM((2, 1024, 1024), BF16),
            pltpu.VMEM((8, 1024, ANG), F32),
            pltpu.VMEM((BOX // 2 * parts, ANG), F32),
            pltpu.VMEM((parts, BOX * BOX), BF16),
            pltpu.VMEM((2, 34 * BOX, 2 * ANG), BF16),
            pltpu.VMEM((CPAD * RAD, ANG), F32),
            pltpu.VMEM((CPAD * RAD, ANG), BF16),
            pltpu.VMEM((ANG, BASE * ANG), BF16),
            pltpu.VMEM((NROWS, cells), BF16),
            pltpu.VMEM((NROWS, ANG), F32),
            pltpu.VMEM((QROT * parts, cells), BF16),
            pltpu.VMEM((NROWS, QROT * parts), F32),
            pltpu.VMEM((NROWS, QROT * parts), BF16),
            pltpu.VMEM((NROWS, ANG), F32),
            pltpu.VMEM((NROWS, 2 * ANG), F32),
            pltpu.VMEM((NROWS, 2 * ANG), F32),
            pltpu.VMEM((2, CHIPS, PIECE, ANG), BF16),
        ]
        + [pltpu.VMEM((CHIPS, PIECE, ANG), BF16)] * 5
        + [pltpu.VMEM((CLASSES * RAD, ANG), F32), pltpu.SemaphoreType.DMA((2,))]
        + [one, pltpu.SemaphoreType.DMA((RAD // 2,)), one, one, one, many, one, many],
        compiler_params=pltpu.CompilerParams(
            vmem_limit_bytes=60 * 1024 * 1024, collective_id=0, has_side_effects=True
        ),
        name="iteration",
    )(positions, counts, micrographs, dest_rows, jnp.asarray(ys), jnp.asarray(xs), templates)
def widen_kernel(means, loglik, wide, same):
    wide[...] = means[...].astype(F32)
    same[...] = loglik[...]


def widen(means, loglik):
    rows = CLASSES * RAD // 4
    return pl.pallas_call(
        widen_kernel,
        grid=(4,),
        out_shape=(
            jax.ShapeDtypeStruct((CLASSES * RAD, ANG), F32),
            jax.ShapeDtypeStruct((1, ANG), F32),
        ),
        in_specs=[pl.BlockSpec((rows, ANG), lambda i: (i, 0)), pl.BlockSpec((1, ANG), lambda i: (0, 0))],
        out_specs=(pl.BlockSpec((rows, ANG), lambda i: (i, 0)), pl.BlockSpec((1, ANG), lambda i: (0, 0))),
        name="widen",
    )(means, loglik)


def on_device(micrographs, positions, counts, dest_rows, templates):
    means, loglik = iteration(micrographs, positions, counts, dest_rows, templates)
    means, loglik = widen(means, loglik)
    return means.reshape(CLASSES, RAD, ANG), loglik.reshape(ANG)


def solution(mesh):
    P = jax.sharding.PartitionSpec
    return jax.shard_map(
        on_device,
        mesh=mesh,
        in_specs=(P("dev", None, None), P(None, "dev", None), P("dev"), P("dev", None), P()),
        out_specs=(P(), P("dev")),
        check_vma=False,
    )
```

```python
import functools
import numpy as np
import jax
import jax.numpy as jnp
from jax import lax
from jax.experimental import pallas as pl
from jax.experimental.pallas import tpu as pltpu

BOX = 64
RAD = 32
ANG = 128
CLASSES = 100
ROTS = 36
CPAD = 104
QROT = 4
BASE = 9
NROWS = 4 * 2 * CPAD + 112
DEVICES = 128
CHIPS = DEVICES // 2
PIECE = 32
F32 = jnp.float32
BF16 = jnp.bfloat16


def sample_points():
    center = np.float32((BOX - 1) / 2.0)
    radius = (np.arange(RAD, dtype=np.float32) + np.float32(0.5)) * np.float32(BOX / 2.0 - 1.0) / np.float32(RAD)
    theta = np.float32(2.0 * np.pi) * np.arange(ANG, dtype=np.float32) / np.float32(ANG)
    ys = (center + radius[:, None] * np.sin(theta)[None, :]).reshape(1, -1)
    xs = (center + radius[:, None] * np.cos(theta)[None, :]).reshape(1, -1)
    def ordered(v):
        v = v.astype(np.float32).reshape(RAD // 4, 2, 2, 2, ANG // 2)
        v = v.transpose(0, 3, 1, 2, 4)
        v = np.stack([v[:, 0], v[:, 1, :, ::-1]], axis=1)
        return v.reshape(1, -1)

    return ordered(ys), ordered(xs)


def rotation_taps():
    a = np.arange(ANG, dtype=np.float32)
    taps = []
    for k in range(BASE):
        shift = np.float32(k) * np.float32(ANG) / np.float32(ROTS)
        d = a - np.float32(0) - shift
        d = d - ANG * np.floor(d / np.float32(ANG) + np.float32(0.5))
        w = np.maximum(np.float32(0), np.float32(1) - np.abs(d)).astype(jnp.bfloat16).astype(np.float32)
        first = int(32 * k // 9)
        taps.append((first, float(w[first]), float(w[(first + 1) % ANG]) if k else 0.0))
    return taps


TAPS = rotation_taps()


def turned_rows(x, i):
    if i == 8:
        return x[8 * CPAD : 9 * CPAD]
    pair = x[(i // 2) * 2 * CPAD : (i // 2 + 1) * 2 * CPAD].reshape(CPAD // 8, 16, x.shape[1])
    return pair[:, 8 * (i % 2) : 8 * (i % 2) + 8].reshape(CPAD, x.shape[1])


def remote(src, dst, send_sem, recv_sem, device):
    return pltpu.make_async_remote_copy(
        src_ref=src,
        dst_ref=dst,
        send_sem=send_sem,
        recv_sem=recv_sem,
        device_id=(device,),
        device_id_type=pl.DeviceIdType.MESH,
    )


def iteration_kernel(pos, counts, mic, dest, ys, xs, tmpl, means, evidence, extra, raw, planes, flat, boxes, wtile, tflat, byrad, rmat, rot, esum, shifted, scores, weights, tsum, sums_a, sums_b, out, half, send, landed, gathered, crossed, table, sems,
                     half_send, half_recv, put_send, put_recv, get_send, get_recv, cross_send, cross_recv):
    mics = mic.shape[0]
    slots = pos.shape[2]
    parts = mics * slots

    me = lax.axis_index("dev")
    core = lax.rem(me, 2)
    chip = me // 2
    partner = me + 1 - 2 * core

    barrier = pltpu.get_barrier_semaphore()
    pl.semaphore_signal(barrier, inc=1, device_id=(partner,), device_id_type=pl.DeviceIdType.MESH)

    def greet(k, _):
        pl.semaphore_signal(
            barrier, inc=1, device_id=(2 * (chip ^ k) + core,), device_id_type=pl.DeviceIdType.MESH
        )
        return 0

    lax.fori_loop(1, CHIPS, greet, 0)

    def fetch(i):
        return pltpu.make_async_copy(mic.at[i], raw.at[i % 2], sems.at[i % 2])

    fetch(0).start()
    fetch(1).start()

    lane1 = lax.broadcasted_iota(jnp.int32, (1, ANG), 1)

    away = lax.broadcasted_iota(jnp.int32, (ANG, ANG), 1) - lax.broadcasted_iota(jnp.int32, (ANG, ANG), 0)
    for i, (first, w0, w1) in enumerate(TAPS):
        step = (away - first) & 127
        turn = jnp.where(step == 0, w0, jnp.where(step == 1, w1, 0.0))
        rmat[:, i * ANG : (i + 1) * ANG] = turn.astype(BF16)
    tflat[pl.ds(CLASSES * RAD, (CPAD - CLASSES) * RAD), :] = jnp.zeros(((CPAD - CLASSES) * RAD, ANG), F32)
    tflat[pl.ds(0, CLASSES * RAD), :] = tmpl[...].reshape(CLASSES * RAD, ANG).astype(F32)
    esum[...] = jnp.zeros_like(esum)
    tiles = CPAD // 8

    def regroup(n, _):
        pair = [tflat[pl.ds(2 * n + h, CPAD, stride=RAD), :] for h in range(2)]
        byrad[pl.ds(pl.multiple_of(n * 2 * CPAD, 16), 2 * CPAD), :] = jnp.concatenate(pair, axis=0).astype(BF16)
        return 0

    lax.fori_loop(0, RAD // 2, regroup, 0, unroll=2)

    def rotate_block(n, _):
        few = 4
        block = byrad[pl.ds(pl.multiple_of(n * few * CPAD, 16), few * CPAD), :]
        for k in range(5):
            start, height = (k * 2 * CPAD, 2 * CPAD) if k < 4 else (8 * CPAD, 112)
            wide = jnp.dot(block, rmat[:, k * 2 * ANG : min(k * 2 + 2, 9) * ANG], preferred_element_type=F32)
            total = jnp.zeros((height, ANG), F32)
            for h in range(few):
                some = wide[h * CPAD : (h + 1) * CPAD]
                if k < 4:
                    some = [some[:, m * ANG : (m + 1) * ANG].reshape(tiles, 8, ANG) for m in range(2)]
                    some = jnp.concatenate(some, axis=1).reshape(2 * CPAD, ANG)
                else:
                    some = jnp.concatenate([some, jnp.zeros((8, ANG), F32)], axis=0)
                some = some.astype(BF16)
                col = pl.ds(pl.multiple_of((n * few + h) * ANG, ANG), ANG)
                rot[start : start + height, col] = some
                some = some.astype(F32)
                total += some * some
            esum[start : start + height, :] += total
        return 0

    lax.fori_loop(0, RAD // 4, rotate_block, 0)

    lanes = lax.broadcasted_iota(jnp.int32, (BOX // 2, ANG), 1)
    for i in range(mics):
        fetch(i).wait()
        for t in range(8):
            planes[t, :, :] = raw[i % 2, :, t * ANG : (t + 1) * ANG].astype(F32)
        if i + 2 < mics:
            fetch(i + 2).start()

        def cut(j, _, i=i):
            y = pos[0, i, j]
            x = pos[1, i, j]
            t = x >> 7
            s = x & 127
            t1 = jnp.minimum(t + 1, 7)
            even = pl.ds(y, BOX // 2, stride=2)
            odd = pl.ds(y + 1, BOX // 2, stride=2)
            keep = lanes >= s
            e = jnp.where(keep, planes[t, even, :], planes[t1, even, :])
            o = jnp.where(keep, planes[t, odd, :], planes[t1, odd, :])
            e = pltpu.roll(e, (ANG - s) & 127, 1)
            o = pltpu.roll(o, (ANG + BOX - s) & 127, 1)
            flat[pl.ds(pl.multiple_of((i * slots + j) * (BOX // 2), BOX // 2), BOX // 2), :] = jnp.where(lanes < BOX, e, o)
            return 0

        lax.fori_loop(0, slots, cut, 0, unroll=16)

    for s in range(BOX // 2):
        boxes[:, s * ANG : (s + 1) * ANG] = flat[pl.ds(s, parts, stride=BOX // 2), :].astype(BF16)

    pix = lax.broadcasted_iota(jnp.int32, (BOX, 2 * ANG), 0).astype(F32)
    left = lax.broadcasted_iota(jnp.int32, (parts, ANG), 1) < BOX
    for g in range(RAD // 4):
        radius = (4 * g + 3.5) * (BOX / 2.0 - 1.0) / RAD
        reach = (int(np.floor(31.501 + radius)) + 3) // 2 * 2
        halves = []
        for side in range(2):
            low, high = (30, reach) if side == 0 else (BOX - reach, 34)
            cols = slice((2 * g + side) * 2 * ANG, (2 * g + side + 1) * 2 * ANG)
            rw = jnp.maximum(0.0, 1.0 - jnp.abs(pix - ys[:, cols]))
            cw = jnp.maximum(0.0, 1.0 - jnp.abs(pix - xs[:, cols]))
            w = wtile.at[side]
            for u in range(low, high):
                w[(u - low) * BOX : (u - low + 1) * BOX, :] = (rw[u : u + 1, :] * cw).astype(BF16)
            halves.append(
                jnp.dot(
                    boxes[:, low * BOX : high * BOX],
                    w[: (high - low) * BOX, :],
                    preferred_element_type=F32,
                )
            )
        for m in range(2):
            upper = halves[0][:, m * ANG : (m + 1) * ANG]
            lower = halves[1][:, m * ANG : (m + 1) * ANG]
            for h in range(2):
                whole = jnp.where(left, upper, lower) if h == 0 else jnp.where(left, lower, upper)
                c0 = (4 * g + 2 * m + h) * ANG
                for j in range(QROT):
                    turn = (BOX * h - 32 * j) % ANG
                    part = pltpu.roll(whole, turn, 1) if turn else whole
                    shifted[j * parts : (j + 1) * parts, c0 : c0 + ANG] = part.astype(BF16)

    spare = [2 * CPAD * k + 8 * h + 196 for k in range(4) for h in range(2)]
    for start in spare:
        esum[start : start + 4, :] = jnp.full((4, ANG), 1e28, F32)
    esum[NROWS - 12 :, :] = jnp.full((12, ANG), 1e28, F32)
    energy = 0.5 * jnp.sum(esum[...], axis=1, keepdims=True)

    def score(j, peak):
        rows_j = pl.ds(pl.multiple_of(j * parts, parts), parts)
        prod = lax.dot_general(rot[...], shifted[rows_j, :], (((1,), (1,)), ((), ())), preferred_element_type=F32)
        prod = prod - energy
        scores[:, rows_j] = prod
        return jnp.maximum(peak, jnp.max(prod, axis=0, keepdims=True))

    peak = lax.fori_loop(0, QROT, score, jnp.full((1, parts), -3e38, F32))
    peak4 = jnp.concatenate([peak] * QROT, axis=1)

    def expo(n, acc):
        rr = pl.ds(pl.multiple_of(n * 16, 16), 16)
        e = jnp.exp(scores[rr, :] - peak4)
        scores[rr, :] = e
        return acc + e[:8] + e[8:]

    def expo_pair(n, acc):
        return expo(2 * n + 1, expo(2 * n, acc))

    acc = lax.fori_loop(0, NROWS // 32, expo_pair, jnp.zeros((8, QROT * parts), F32))
    acc = expo(NROWS // 16 - 1, acc)
    norm = jnp.sum(acc, axis=0, keepdims=True)
    norm = sum(norm[:, j * parts : (j + 1) * parts] for j in range(QROT))
    loglik = peak + jnp.log(norm)

    lane = lax.broadcasted_iota(jnp.int32, (1, parts), 1)
    target = jnp.concatenate([dest[i : i + 1, :] for i in range(mics)], axis=1)
    live = target >= 0
    for i in range(mics):
        live = live & ((lane < i * slots + counts[i]) | (lane >= (i + 1) * slots))
    inv = jnp.where(live, 1.0 / norm, 0.0)
    inv4 = jnp.concatenate([inv] * QROT, axis=1)

    def weigh(n, _):
        rr = pl.ds(pl.multiple_of(n * 16, 16), 16)
        w = (scores[rr, :] * inv4).astype(BF16)
        weights[rr, :] = w
        wide = w.astype(F32)
        tsum[rr, :] = sum(wide[:, k * ANG : (k + 1) * ANG] for k in range(QROT * parts // ANG))
        return 0

    def weigh_pair(n, _):
        weigh(2 * n, 0)
        return weigh(2 * n + 1, 0)

    lax.fori_loop(0, NROWS // 32, weigh_pair, 0)
    weigh(NROWS // 16 - 1, 0)
    tot = jnp.sum(sum(turned_rows(tsum[...], i) for i in range(BASE)), axis=1, keepdims=True)
    spot = lax.broadcasted_iota(jnp.int32, (CPAD, ANG), 0) == lax.broadcasted_iota(jnp.int32, (CPAD, ANG), 1)
    tot = jnp.sum(jnp.where(spot, tot, 0.0), axis=0, keepdims=True)
    high = tot.astype(BF16).astype(F32)
    first = core == 0
    extra[...] = jnp.zeros_like(extra)
    for value, here, there in ((high, 1, 6), (tot - high, 2, 7)):
        value = jnp.broadcast_to(value, (DEVICES, ANG))
        extra[pl.ds(here, DEVICES, stride=8), :] = jnp.where(first, value, 0.0)
        extra[pl.ds(there, DEVICES, stride=8), :] = jnp.where(first, 0.0, value)

    which = lax.broadcasted_iota(jnp.int32, (ANG, parts), 0)
    owner = jnp.where((which == (target >> 7)) & live, 1.0, 0.0)
    row = jnp.where(which == (target & 127), 1.0, 0.0).astype(BF16)
    rest = loglik
    for k in range(3):
        piece = rest.astype(BF16).astype(F32)
        placed = lax.dot_general((owner * piece).astype(BF16), row, (((1,), (1,)), ((), ())), preferred_element_type=F32)
        extra[pl.ds(3 + k, DEVICES, stride=8), :] = placed
        rest = rest - piece

    top = lax.broadcasted_iota(jnp.int32, (8, ANG), 0)

    def turn(n):
        return (RAD // 2 - 1 - n) ^ (chip // 4)

    def product(n, into):
        g = turn(n)
        cols = pl.ds(pl.multiple_of(g * 2 * ANG, 2 * ANG), 2 * ANG)
        into[...] = jnp.dot(weights[...], shifted[:, cols], preferred_element_type=F32)

    def fold(n, source):
        g = turn(n)
        for k in range(2):
            sum0 = jnp.zeros((CPAD, ANG), F32)
            sum1 = jnp.zeros((CPAD, ANG), F32)
            half = source[:, k * ANG : (k + 1) * ANG]
            for i, (first, w0, w1) in enumerate(TAPS):
                q = turned_rows(half, i)
                if first:
                    q = pltpu.roll(q, ANG - first, 1)
                sum0 += w0 * q
                if w1:
                    sum1 += w1 * q
            total = sum0 + pltpu.roll(sum1, ANG - 1, 1)
            r = 2 * g + k
            for q in range(4):
                tail = total[96:] if q == 0 else pltpu.roll(total[96:], 8 - q, 0)
                spare = extra[pl.ds(pl.multiple_of((4 * r + q) * 8, 8), 8), :]
                tail = jnp.where(top == 0, tail, spare)
                piece = jnp.concatenate([total[24 * q : 24 * q + 24], tail], axis=0)
                out[q % 2, 2 * r + q // 2, :, :] = piece.astype(BF16)

    def half_copy(n):
        at = pl.ds(4 * turn(n), 4)
        return remote(out.at[1 - core, at], half.at[at], half_send, half_recv.at[n], partner)

    def put(c):
        return remote(send.at[c], landed.at[chip], put_send, put_recv, 2 * c + core)

    def give(n, home=False):
        half_copy(n).wait_recv()
        for m in range(4):
            c = 4 * turn(n) + m
            send[c] = (out[core, c].astype(F32) + half[c].astype(F32)).astype(BF16)
        if home:
            landed[chip] = send[chip]
        for m in range(4):
            c = 4 * turn(n) + m
            if home:

                @pl.when(c != chip)
                def _():
                    put(c).start()

            else:
                put(c).start()

    def pair(n):
        product(2 * n + 1, sums_b)
        fold(2 * n, sums_a)
        product(2 * n + 2, sums_a)
        fold(2 * n + 1, sums_b)
        half_copy(2 * n).start()
        half_copy(2 * n + 1).start()

    def alone(n, _):
        pair(n)
        return 0

    def sending(n, _):
        pair(n)
        give(2 * n - 2)
        give(2 * n - 1)
        return 0

    last = RAD // 2 - 1
    product(0, sums_a)
    pl.semaphore_wait(barrier, CHIPS)
    lax.fori_loop(0, 2, alone, 0)
    give(0)
    give(1)
    lax.fori_loop(2, last // 2, sending, 0)
    product(last, sums_b)
    fold(last - 1, sums_a)
    half_copy(last - 1).start()
    give(last - 3)
    give(last - 2)
    fold(last, sums_b)
    half_copy(last).start()
    give(last - 1)
    give(last, home=True)

    others = pl.ds(0, CHIPS - 1)
    remote(send.at[others], landed.at[others], put_send, put_recv, partner).wait_recv()

    def take(k, acc):
        return acc + sum(landed[8 * k + m].astype(F32) for m in range(8))

    acc = lax.fori_loop(0, CHIPS // 8, take, jnp.zeros((PIECE, ANG), F32))

    quarter = 2 * lax.rem(chip, 2) + core
    row = lax.broadcasted_iota(jnp.int32, (PIECE, ANG), 0)
    lane = lax.broadcasted_iota(jnp.int32, (PIECE, ANG), 1)
    which = jnp.where(row < 24, 24 * quarter + row, 96 + quarter)
    total = acc[25:26] + acc[26:27] + acc[30:31] + acc[31:32]
    total = jnp.sum(jnp.where(lane == which, total, 0.0), axis=1, keepdims=True)
    gathered[chip] = (acc / jnp.maximum(total, 1.0)).astype(BF16)
    evidence[...] = acc[27:28] + acc[28:29] + acc[29:30]

    def share(slot, to):
        return remote(gathered.at[slot], gathered.at[slot], get_send, get_recv.at[slot], 2 * to + core)

    def pass_on(c):
        return remote(gathered.at[c], crossed.at[c], cross_send, cross_recv.at[c], partner)

    def spread(k, _):
        share(chip, chip ^ k ^ 42).start()
        return 0

    lax.fori_loop(0, 42, spread, 0, unroll=3)
    lax.fori_loop(43, CHIPS, spread, 0, unroll=3)
    pass_on(chip).start()

    def write(piece, c, k):
        r = c // 2
        q = 2 * lax.rem(c, 2) + k
        wide = piece.astype(F32)
        table[pl.ds(24 * RAD * q + r, 24, stride=RAD), :] = wide[:24]
        table[pl.ds((96 + q) * RAD + r, 1), :] = wide[24:25]

    def cross(k):
        c = chip ^ k
        pass_on(c).wait_recv()
        write(crossed[c], c, 1 - core)

    def pick(k):
        c = chip ^ k
        share(c, c).wait_recv()
        pass_on(c).start()
        write(gathered[c], c, core)

    lag = 6
    write(gathered[chip], chip, core)

    def early(k, _):
        pick(k)
        return 0

    def both(k, _):
        pick(k)
        cross(k - lag)
        return 0

    def late(k, _):
        cross(k)
        return 0

    lax.fori_loop(1, lag, early, 0)
    lax.fori_loop(lag, CHIPS, both, 0)
    lax.fori_loop(CHIPS - lag, CHIPS, late, 0)
    means[...] = table[...].astype(BF16)

    remote(out.at[1 - core], half, half_send, half_recv.at[0], partner).wait_send()
    remote(send.at[others], landed.at[others], put_send, put_recv, partner).wait_send()
    remote(gathered.at[others], landed.at[others], get_send, put_recv, partner).wait_send()
    remote(gathered, crossed, cross_send, put_recv, partner).wait_send()


def iteration(micrographs, positions, counts, dest_rows, templates):
    mics, slots = dest_rows.shape
    parts = mics * slots
    cells = RAD * ANG
    ys, xs = sample_points()
    vmem = pl.BlockSpec(memory_space=pltpu.VMEM)
    smem = pl.BlockSpec(memory_space=pltpu.SMEM)
    one = pltpu.SemaphoreType.DMA
    many = pltpu.SemaphoreType.DMA((CHIPS,))
    return pl.pallas_call(
        iteration_kernel,
        out_shape=(
            jax.ShapeDtypeStruct((CLASSES * RAD, ANG), BF16),
            jax.ShapeDtypeStruct((1, ANG), F32),
        ),
        in_specs=[smem, smem, pl.BlockSpec(memory_space=pl.ANY), vmem, vmem, vmem, vmem],
        out_specs=(vmem, vmem),
        scratch_shapes=[
            pltpu.VMEM((DEVICES * 8, ANG), F32),
            pltpu.VMEM((2, 1024, 1024), BF16),
            pltpu.VMEM((8, 1024, ANG), F32),
            pltpu.VMEM((BOX // 2 * parts, ANG), F32),
            pltpu.VMEM((parts, BOX * BOX), BF16),
            pltpu.VMEM((2, 34 * BOX, 2 * ANG), BF16),
            pltpu.VMEM((CPAD * RAD, ANG), F32),
            pltpu.VMEM((CPAD * RAD, ANG), BF16),
            pltpu.VMEM((ANG, BASE * ANG), BF16),
            pltpu.VMEM((NROWS, cells), BF16),
            pltpu.VMEM((NROWS, ANG), F32),
            pltpu.VMEM((QROT * parts, cells), BF16),
            pltpu.VMEM((NROWS, QROT * parts), F32),
            pltpu.VMEM((NROWS, QROT * parts), BF16),
            pltpu.VMEM((NROWS, ANG), F32),
            pltpu.VMEM((NROWS, 2 * ANG), F32),
            pltpu.VMEM((NROWS, 2 * ANG), F32),
            pltpu.VMEM((2, CHIPS, PIECE, ANG), BF16),
        ]
        + [pltpu.VMEM((CHIPS, PIECE, ANG), BF16)] * 5
        + [pltpu.VMEM((CLASSES * RAD, ANG), F32), pltpu.SemaphoreType.DMA((2,))]
        + [one, pltpu.SemaphoreType.DMA((RAD // 2,)), one, one, one, many, one, many],
        compiler_params=pltpu.CompilerParams(
            vmem_limit_bytes=60 * 1024 * 1024, collective_id=0, has_side_effects=True
        ),
        name="iteration",
    )(positions, counts, micrographs, dest_rows, jnp.asarray(ys), jnp.asarray(xs), templates)
def widen_kernel(means, loglik, wide, same):
    wide[...] = means[...].astype(F32)
    same[...] = loglik[...]


def widen(means, loglik):
    rows = CLASSES * RAD // 2
    return pl.pallas_call(
        widen_kernel,
        grid=(2,),
        out_shape=(
            jax.ShapeDtypeStruct((CLASSES * RAD, ANG), F32),
            jax.ShapeDtypeStruct((1, ANG), F32),
        ),
        in_specs=[pl.BlockSpec((rows, ANG), lambda i: (i, 0)), pl.BlockSpec((1, ANG), lambda i: (0, 0))],
        out_specs=(pl.BlockSpec((rows, ANG), lambda i: (i, 0)), pl.BlockSpec((1, ANG), lambda i: (0, 0))),
        name="widen",
    )(means, loglik)


def on_device(micrographs, positions, counts, dest_rows, templates):
    means, loglik = iteration(micrographs, positions, counts, dest_rows, templates)
    means, loglik = widen(means, loglik)
    return means.reshape(CLASSES, RAD, ANG), loglik.reshape(ANG)


def solution(mesh):
    P = jax.sharding.PartitionSpec
    return jax.shard_map(
        on_device,
        mesh=mesh,
        in_specs=(P("dev", None, None), P(None, "dev", None), P("dev"), P("dev", None), P()),
        out_specs=(P(), P("dev")),
        check_vma=False,
    )
```

```python
import functools
import numpy as np
import jax
import jax.numpy as jnp
from jax import lax
from jax.experimental import pallas as pl
from jax.experimental.pallas import tpu as pltpu

BOX = 64
RAD = 32
ANG = 128
CLASSES = 100
ROTS = 36
CPAD = 104
QROT = 4
BASE = 9
NROWS = 4 * 2 * CPAD + 112
DEVICES = 128
CHIPS = DEVICES // 2
PIECE = 32
F32 = jnp.float32
BF16 = jnp.bfloat16


def sample_points():
    center = np.float32((BOX - 1) / 2.0)
    radius = (np.arange(RAD, dtype=np.float32) + np.float32(0.5)) * np.float32(BOX / 2.0 - 1.0) / np.float32(RAD)
    theta = np.float32(2.0 * np.pi) * np.arange(ANG, dtype=np.float32) / np.float32(ANG)
    ys = (center + radius[:, None] * np.sin(theta)[None, :]).reshape(1, -1)
    xs = (center + radius[:, None] * np.cos(theta)[None, :]).reshape(1, -1)
    def ordered(v):
        v = v.astype(np.float32).reshape(RAD // 4, 2, 2, 2, ANG // 2)
        v = v.transpose(0, 3, 1, 2, 4)
        v = np.stack([v[:, 0], v[:, 1, :, ::-1]], axis=1)
        return v.reshape(1, -1)

    return ordered(ys), ordered(xs)


def rotation_taps():
    a = np.arange(ANG, dtype=np.float32)
    taps = []
    for k in range(BASE):
        shift = np.float32(k) * np.float32(ANG) / np.float32(ROTS)
        d = a - np.float32(0) - shift
        d = d - ANG * np.floor(d / np.float32(ANG) + np.float32(0.5))
        w = np.maximum(np.float32(0), np.float32(1) - np.abs(d)).astype(jnp.bfloat16).astype(np.float32)
        first = int(32 * k // 9)
        taps.append((first, float(w[first]), float(w[(first + 1) % ANG]) if k else 0.0))
    return taps


TAPS = rotation_taps()


def turned_rows(x, i):
    if i == 8:
        return x[8 * CPAD : 9 * CPAD]
    pair = x[(i // 2) * 2 * CPAD : (i // 2 + 1) * 2 * CPAD].reshape(CPAD // 8, 16, x.shape[1])
    return pair[:, 8 * (i % 2) : 8 * (i % 2) + 8].reshape(CPAD, x.shape[1])


def remote(src, dst, send_sem, recv_sem, device):
    return pltpu.make_async_remote_copy(
        src_ref=src,
        dst_ref=dst,
        send_sem=send_sem,
        recv_sem=recv_sem,
        device_id=(device,),
        device_id_type=pl.DeviceIdType.MESH,
    )


def iteration_kernel(pos, counts, mic, dest, ys, xs, tmpl, means, evidence, extra, raw, planes, flat, boxes, wtile, tflat, byrad, rmat, rot, esum, shifted, scores, weights, tsum, sums_a, sums_b, out, half, send, landed, gathered, crossed, table, sems,
                     half_send, half_recv, put_send, put_recv, get_send, get_recv, cross_send, cross_recv):
    mics = mic.shape[0]
    slots = pos.shape[2]
    parts = mics * slots

    me = lax.axis_index("dev")
    core = lax.rem(me, 2)
    chip = me // 2
    partner = me + 1 - 2 * core

    barrier = pltpu.get_barrier_semaphore()
    pl.semaphore_signal(barrier, inc=1, device_id=(partner,), device_id_type=pl.DeviceIdType.MESH)

    def greet(k, _):
        pl.semaphore_signal(
            barrier, inc=1, device_id=(2 * (chip ^ k) + core,), device_id_type=pl.DeviceIdType.MESH
        )
        return 0

    lax.fori_loop(1, CHIPS, greet, 0)

    def fetch(i):
        return pltpu.make_async_copy(mic.at[i], raw.at[i % 2], sems.at[i % 2])

    fetch(0).start()
    fetch(1).start()

    lane1 = lax.broadcasted_iota(jnp.int32, (1, ANG), 1)

    away = lax.broadcasted_iota(jnp.int32, (ANG, ANG), 1) - lax.broadcasted_iota(jnp.int32, (ANG, ANG), 0)
    for i, (first, w0, w1) in enumerate(TAPS):
        step = (away - first) & 127
        turn = jnp.where(step == 0, w0, jnp.where(step == 1, w1, 0.0))
        rmat[:, i * ANG : (i + 1) * ANG] = turn.astype(BF16)
    tflat[pl.ds(CLASSES * RAD, (CPAD - CLASSES) * RAD), :] = jnp.zeros(((CPAD - CLASSES) * RAD, ANG), F32)
    tflat[pl.ds(0, CLASSES * RAD), :] = tmpl[...].reshape(CLASSES * RAD, ANG).astype(F32)
    esum[...] = jnp.zeros_like(esum)
    tiles = CPAD // 8

    def regroup(n, _):
        pair = [tflat[pl.ds(2 * n + h, CPAD, stride=RAD), :] for h in range(2)]
        byrad[pl.ds(pl.multiple_of(n * 2 * CPAD, 16), 2 * CPAD), :] = jnp.concatenate(pair, axis=0).astype(BF16)
        return 0

    lax.fori_loop(0, RAD // 2, regroup, 0, unroll=2)

    def rotate_block(n, _):
        few = 8
        block = byrad[pl.ds(pl.multiple_of(n * few * CPAD, 16), few * CPAD), :]
        for k in range(5):
            start, height = (k * 2 * CPAD, 2 * CPAD) if k < 4 else (8 * CPAD, 112)
            wide = jnp.dot(block, rmat[:, k * 2 * ANG : min(k * 2 + 2, 9) * ANG], preferred_element_type=F32)
            total = jnp.zeros((height, ANG), F32)
            for h in range(few):
                some = wide[h * CPAD : (h + 1) * CPAD]
                if k < 4:
                    some = [some[:, m * ANG : (m + 1) * ANG].reshape(tiles, 8, ANG) for m in range(2)]
                    some = jnp.concatenate(some, axis=1).reshape(2 * CPAD, ANG)
                else:
                    some = jnp.concatenate([some, jnp.zeros((8, ANG), F32)], axis=0)
                some = some.astype(BF16)
                col = pl.ds(pl.multiple_of((n * few + h) * ANG, ANG), ANG)
                rot[start : start + height, col] = some
                some = some.astype(F32)
                total += some * some
            esum[start : start + height, :] += total
        return 0

    lax.fori_loop(0, RAD // 8, rotate_block, 0)

    lanes = lax.broadcasted_iota(jnp.int32, (BOX // 2, ANG), 1)
    for i in range(mics):
        fetch(i).wait()
        for t in range(8):
            planes[t, :, :] = raw[i % 2, :, t * ANG : (t + 1) * ANG].astype(F32)
        if i + 2 < mics:
            fetch(i + 2).start()

        def cut(j, _, i=i):
            y = pos[0, i, j]
            x = pos[1, i, j]
            t = x >> 7
            s = x & 127
            t1 = jnp.minimum(t + 1, 7)
            even = pl.ds(y, BOX // 2, stride=2)
            odd = pl.ds(y + 1, BOX // 2, stride=2)
            keep = lanes >= s
            e = jnp.where(keep, planes[t, even, :], planes[t1, even, :])
            o = jnp.where(keep, planes[t, odd, :], planes[t1, odd, :])
            e = pltpu.roll(e, (ANG - s) & 127, 1)
            o = pltpu.roll(o, (ANG + BOX - s) & 127, 1)
            flat[pl.ds(pl.multiple_of((i * slots + j) * (BOX // 2), BOX // 2), BOX // 2), :] = jnp.where(lanes < BOX, e, o)
            return 0

        lax.fori_loop(0, slots, cut, 0, unroll=32)

    for s in range(BOX // 2):
        boxes[:, s * ANG : (s + 1) * ANG] = flat[pl.ds(s, parts, stride=BOX // 2), :].astype(BF16)

    pix = lax.broadcasted_iota(jnp.int32, (BOX, 2 * ANG), 0).astype(F32)
    left = lax.broadcasted_iota(jnp.int32, (parts, ANG), 1) < BOX
    for g in range(RAD // 4):
        radius = (4 * g + 3.5) * (BOX / 2.0 - 1.0) / RAD
        reach = (int(np.floor(31.501 + radius)) + 3) // 2 * 2
        halves = []
        for side in range(2):
            low, high = (30, reach) if side == 0 else (BOX - reach, 34)
            cols = slice((2 * g + side) * 2 * ANG, (2 * g + side + 1) * 2 * ANG)
            rw = jnp.maximum(0.0, 1.0 - jnp.abs(pix - ys[:, cols]))
            cw = jnp.maximum(0.0, 1.0 - jnp.abs(pix - xs[:, cols]))
            w = wtile.at[side]
            for u in range(low, high):
                w[(u - low) * BOX : (u - low + 1) * BOX, :] = (rw[u : u + 1, :] * cw).astype(BF16)
            halves.append(
                jnp.dot(
                    boxes[:, low * BOX : high * BOX],
                    w[: (high - low) * BOX, :],
                    preferred_element_type=F32,
                )
            )
        for m in range(2):
            upper = halves[0][:, m * ANG : (m + 1) * ANG]
            lower = halves[1][:, m * ANG : (m + 1) * ANG]
            for h in range(2):
                whole = jnp.where(left, upper, lower) if h == 0 else jnp.where(left, lower, upper)
                c0 = (4 * g + 2 * m + h) * ANG
                for j in range(QROT):
                    turn = (BOX * h - 32 * j) % ANG
                    part = pltpu.roll(whole, turn, 1) if turn else whole
                    shifted[j * parts : (j + 1) * parts, c0 : c0 + ANG] = part.astype(BF16)

    spare = [2 * CPAD * k + 8 * h + 196 for k in range(4) for h in range(2)]
    for start in spare:
        esum[start : start + 4, :] = jnp.full((4, ANG), 1e28, F32)
    esum[NROWS - 12 :, :] = jnp.full((12, ANG), 1e28, F32)
    energy = 0.5 * jnp.sum(esum[...], axis=1, keepdims=True)

    def score(j, peak):
        rows_j = pl.ds(pl.multiple_of(j * parts, parts), parts)
        prod = lax.dot_general(rot[...], shifted[rows_j, :], (((1,), (1,)), ((), ())), preferred_element_type=F32)
        prod = prod - energy
        scores[:, rows_j] = prod
        return jnp.maximum(peak, jnp.max(prod, axis=0, keepdims=True))

    peak = lax.fori_loop(0, QROT, score, jnp.full((1, parts), -3e38, F32))
    peak4 = jnp.concatenate([peak] * QROT, axis=1)

    def expo(n, acc):
        rr = pl.ds(pl.multiple_of(n * 16, 16), 16)
        e = jnp.exp(scores[rr, :] - peak4)
        scores[rr, :] = e
        return acc + e[:8] + e[8:]

    def expo_pair(n, acc):
        return expo(2 * n + 1, expo(2 * n, acc))

    acc = lax.fori_loop(0, NROWS // 32, expo_pair, jnp.zeros((8, QROT * parts), F32))
    acc = expo(NROWS // 16 - 1, acc)
    norm = jnp.sum(acc, axis=0, keepdims=True)
    norm = sum(norm[:, j * parts : (j + 1) * parts] for j in range(QROT))
    loglik = peak + jnp.log(norm)

    lane = lax.broadcasted_iota(jnp.int32, (1, parts), 1)
    target = jnp.concatenate([dest[i : i + 1, :] for i in range(mics)], axis=1)
    live = target >= 0
    for i in range(mics):
        live = live & ((lane < i * slots + counts[i]) | (lane >= (i + 1) * slots))
    inv = jnp.where(live, 1.0 / norm, 0.0)
    inv4 = jnp.concatenate([inv] * QROT, axis=1)

    def weigh(n, _):
        rr = pl.ds(pl.multiple_of(n * 16, 16), 16)
        w = (scores[rr, :] * inv4).astype(BF16)
        weights[rr, :] = w
        wide = w.astype(F32)
        tsum[rr, :] = sum(wide[:, k * ANG : (k + 1) * ANG] for k in range(QROT * parts // ANG))
        return 0

    def weigh_pair(n, _):
        weigh(2 * n, 0)
        return weigh(2 * n + 1, 0)

    lax.fori_loop(0, NROWS // 32, weigh_pair, 0)
    weigh(NROWS // 16 - 1, 0)
    tot = jnp.sum(sum(turned_rows(tsum[...], i) for i in range(BASE)), axis=1, keepdims=True)
    spot = lax.broadcasted_iota(jnp.int32, (CPAD, ANG), 0) == lax.broadcasted_iota(jnp.int32, (CPAD, ANG), 1)
    tot = jnp.sum(jnp.where(spot, tot, 0.0), axis=0, keepdims=True)
    high = tot.astype(BF16).astype(F32)
    first = core == 0
    extra[...] = jnp.zeros_like(extra)
    for value, here, there in ((high, 1, 6), (tot - high, 2, 7)):
        value = jnp.broadcast_to(value, (DEVICES, ANG))
        extra[pl.ds(here, DEVICES, stride=8), :] = jnp.where(first, value, 0.0)
        extra[pl.ds(there, DEVICES, stride=8), :] = jnp.where(first, 0.0, value)

    which = lax.broadcasted_iota(jnp.int32, (ANG, parts), 0)
    owner = jnp.where((which == (target >> 7)) & live, 1.0, 0.0)
    row = jnp.where(which == (target & 127), 1.0, 0.0).astype(BF16)
    rest = loglik
    for k in range(3):
        piece = rest.astype(BF16).astype(F32)
        placed = lax.dot_general((owner * piece).astype(BF16), row, (((1,), (1,)), ((), ())), preferred_element_type=F32)
        extra[pl.ds(3 + k, DEVICES, stride=8), :] = placed
        rest = rest - piece

    top = lax.broadcasted_iota(jnp.int32, (8, ANG), 0)

    def turn(n):
        return (RAD // 2 - 1 - n) ^ (chip // 4)

    def product(n, into):
        g = turn(n)
        cols = pl.ds(pl.multiple_of(g * 2 * ANG, 2 * ANG), 2 * ANG)
        into[...] = jnp.dot(weights[...], shifted[:, cols], preferred_element_type=F32)

    def fold(n, source):
        g = turn(n)
        for k in range(2):
            sum0 = jnp.zeros((CPAD, ANG), F32)
            sum1 = jnp.zeros((CPAD, ANG), F32)
            half = source[:, k * ANG : (k + 1) * ANG]
            for i, (first, w0, w1) in enumerate(TAPS):
                q = turned_rows(half, i)
                if first:
                    q = pltpu.roll(q, ANG - first, 1)
                sum0 += w0 * q
                if w1:
                    sum1 += w1 * q
            total = sum0 + pltpu.roll(sum1, ANG - 1, 1)
            r = 2 * g + k
            for q in range(4):
                tail = total[96:] if q == 0 else pltpu.roll(total[96:], 8 - q, 0)
                spare = extra[pl.ds(pl.multiple_of((4 * r + q) * 8, 8), 8), :]
                tail = jnp.where(top == 0, tail, spare)
                piece = jnp.concatenate([total[24 * q : 24 * q + 24], tail], axis=0)
                out[q % 2, 2 * r + q // 2, :, :] = piece.astype(BF16)

    def half_copy(n):
        at = pl.ds(4 * turn(n), 4)
        return remote(out.at[1 - core, at], half.at[at], half_send, half_recv.at[n], partner)

    def put(c):
        return remote(send.at[c], landed.at[chip], put_send, put_recv, 2 * c + core)

    def give(n, home=False):
        half_copy(n).wait_recv()
        for m in range(4):
            c = 4 * turn(n) + m
            send[c] = (out[core, c].astype(F32) + half[c].astype(F32)).astype(BF16)
        if home:
            landed[chip] = send[chip]
        for m in range(4):
            c = 4 * turn(n) + m
            if home:

                @pl.when(c != chip)
                def _():
                    put(c).start()

            else:
                put(c).start()

    def pair(n):
        product(2 * n + 1, sums_b)
        fold(2 * n, sums_a)
        product(2 * n + 2, sums_a)
        fold(2 * n + 1, sums_b)
        half_copy(2 * n).start()
        half_copy(2 * n + 1).start()

    def alone(n, _):
        pair(n)
        return 0

    def sending(n, _):
        pair(n)
        give(2 * n - 2)
        give(2 * n - 1)
        return 0

    last = RAD // 2 - 1
    product(0, sums_a)
    pl.semaphore_wait(barrier, CHIPS)
    lax.fori_loop(0, 2, alone, 0)
    give(0)
    give(1)
    lax.fori_loop(2, last // 2, sending, 0)
    product(last, sums_b)
    fold(last - 1, sums_a)
    half_copy(last - 1).start()
    give(last - 3)
    give(last - 2)
    fold(last, sums_b)
    half_copy(last).start()
    give(last - 1)
    give(last, home=True)

    others = pl.ds(0, CHIPS - 1)
    remote(send.at[others], landed.at[others], put_send, put_recv, partner).wait_recv()

    def take(k, acc):
        return acc + sum(landed[8 * k + m].astype(F32) for m in range(8))

    acc = lax.fori_loop(0, CHIPS // 8, take, jnp.zeros((PIECE, ANG), F32))

    quarter = 2 * lax.rem(chip, 2) + core
    row = lax.broadcasted_iota(jnp.int32, (PIECE, ANG), 0)
    lane = lax.broadcasted_iota(jnp.int32, (PIECE, ANG), 1)
    which = jnp.where(row < 24, 24 * quarter + row, 96 + quarter)
    total = acc[25:26] + acc[26:27] + acc[30:31] + acc[31:32]
    total = jnp.sum(jnp.where(lane == which, total, 0.0), axis=1, keepdims=True)
    gathered[chip] = (acc / jnp.maximum(total, 1.0)).astype(BF16)
    evidence[...] = acc[27:28] + acc[28:29] + acc[29:30]

    def share(slot, to):
        return remote(gathered.at[slot], gathered.at[slot], get_send, get_recv.at[slot], 2 * to + core)

    def pass_on(c):
        return remote(gathered.at[c], crossed.at[c], cross_send, cross_recv.at[c], partner)

    def spread(k, _):
        share(chip, chip ^ k ^ 42).start()
        return 0

    lax.fori_loop(0, 42, spread, 0, unroll=3)
    lax.fori_loop(43, CHIPS, spread, 0, unroll=3)
    pass_on(chip).start()

    def write(piece, c, k):
        r = c // 2
        q = 2 * lax.rem(c, 2) + k
        wide = piece.astype(F32)
        table[pl.ds(24 * RAD * q + r, 24, stride=RAD), :] = wide[:24]
        table[pl.ds((96 + q) * RAD + r, 1), :] = wide[24:25]

    def cross(k):
        c = chip ^ k
        pass_on(c).wait_recv()
        write(crossed[c], c, 1 - core)

    def pick(k):
        c = chip ^ k
        share(c, c).wait_recv()
        pass_on(c).start()
        write(gathered[c], c, core)

    lag = 6
    write(gathered[chip], chip, core)

    def early(k, _):
        pick(k)
        return 0

    def both(k, _):
        pick(k)
        cross(k - lag)
        return 0

    def late(k, _):
        cross(k)
        return 0

    lax.fori_loop(1, lag, early, 0)
    lax.fori_loop(lag, CHIPS, both, 0)
    lax.fori_loop(CHIPS - lag, CHIPS, late, 0)
    means[...] = table[...].astype(BF16)

    remote(out.at[1 - core], half, half_send, half_recv.at[0], partner).wait_send()
    remote(send.at[others], landed.at[others], put_send, put_recv, partner).wait_send()
    remote(gathered.at[others], landed.at[others], get_send, put_recv, partner).wait_send()
    remote(gathered, crossed, cross_send, put_recv, partner).wait_send()


def iteration(micrographs, positions, counts, dest_rows, templates):
    mics, slots = dest_rows.shape
    parts = mics * slots
    cells = RAD * ANG
    ys, xs = sample_points()
    vmem = pl.BlockSpec(memory_space=pltpu.VMEM)
    smem = pl.BlockSpec(memory_space=pltpu.SMEM)
    one = pltpu.SemaphoreType.DMA
    many = pltpu.SemaphoreType.DMA((CHIPS,))
    return pl.pallas_call(
        iteration_kernel,
        out_shape=(
            jax.ShapeDtypeStruct((CLASSES * RAD, ANG), BF16),
            jax.ShapeDtypeStruct((1, ANG), F32),
        ),
        in_specs=[smem, smem, pl.BlockSpec(memory_space=pl.ANY), vmem, vmem, vmem, vmem],
        out_specs=(vmem, vmem),
        scratch_shapes=[
            pltpu.VMEM((DEVICES * 8, ANG), F32),
            pltpu.VMEM((2, 1024, 1024), BF16),
            pltpu.VMEM((8, 1024, ANG), F32),
            pltpu.VMEM((BOX // 2 * parts, ANG), F32),
            pltpu.VMEM((parts, BOX * BOX), BF16),
            pltpu.VMEM((2, 34 * BOX, 2 * ANG), BF16),
            pltpu.VMEM((CPAD * RAD, ANG), F32),
            pltpu.VMEM((CPAD * RAD, ANG), BF16),
            pltpu.VMEM((ANG, BASE * ANG), BF16),
            pltpu.VMEM((NROWS, cells), BF16),
            pltpu.VMEM((NROWS, ANG), F32),
            pltpu.VMEM((QROT * parts, cells), BF16),
            pltpu.VMEM((NROWS, QROT * parts), F32),
            pltpu.VMEM((NROWS, QROT * parts), BF16),
            pltpu.VMEM((NROWS, ANG), F32),
            pltpu.VMEM((NROWS, 2 * ANG), F32),
            pltpu.VMEM((NROWS, 2 * ANG), F32),
            pltpu.VMEM((2, CHIPS, PIECE, ANG), BF16),
        ]
        + [pltpu.VMEM((CHIPS, PIECE, ANG), BF16)] * 5
        + [pltpu.VMEM((CLASSES * RAD, ANG), F32), pltpu.SemaphoreType.DMA((2,))]
        + [one, pltpu.SemaphoreType.DMA((RAD // 2,)), one, one, one, many, one, many],
        compiler_params=pltpu.CompilerParams(
            vmem_limit_bytes=60 * 1024 * 1024, collective_id=0, has_side_effects=True
        ),
        name="iteration",
    )(positions, counts, micrographs, dest_rows, jnp.asarray(ys), jnp.asarray(xs), templates)
def widen_kernel(means, loglik, wide, same):
    wide[...] = means[...].astype(F32)
    same[...] = loglik[...]


def widen(means, loglik):
    rows = CLASSES * RAD // 2
    return pl.pallas_call(
        widen_kernel,
        grid=(2,),
        out_shape=(
            jax.ShapeDtypeStruct((CLASSES * RAD, ANG), F32),
            jax.ShapeDtypeStruct((1, ANG), F32),
        ),
        in_specs=[pl.BlockSpec((rows, ANG), lambda i: (i, 0)), pl.BlockSpec((1, ANG), lambda i: (0, 0))],
        out_specs=(pl.BlockSpec((rows, ANG), lambda i: (i, 0)), pl.BlockSpec((1, ANG), lambda i: (0, 0))),
        name="widen",
    )(means, loglik)


def on_device(micrographs, positions, counts, dest_rows, templates):
    means, loglik = iteration(micrographs, positions, counts, dest_rows, templates)
    means, loglik = widen(means, loglik)
    return means.reshape(CLASSES, RAD, ANG), loglik.reshape(ANG)


def solution(mesh):
    P = jax.sharding.PartitionSpec
    return jax.shard_map(
        on_device,
        mesh=mesh,
        in_specs=(P("dev", None, None), P(None, "dev", None), P("dev"), P("dev", None), P()),
        out_specs=(P(), P("dev")),
        check_vma=False,
    )
```
